32 devices in a mesh: batch: 2 (over x), strip: 8 (over z, y), plate: 2 (over core).
Axes of the slice: x: 2, y: 2, z: 4, core: 2. Of those that a mesh axis runs over, the one named last changes fastest.
Arguments:
- fields: bfloat16 [32, 1088, 5, 1080], P(('batch', 'strip', 'plate')), parts along dimension 0, may hold values from 0.05 to 80, as said below
- flat_gain: bfloat16 [1088, 5, 1080], P('strip'), may hold values from 0.5 to 1.5
Outputs:
- corrected: bfloat16 [32, 1088, 5, 1080], P(('batch', 'strip', 'plate')), parts along dimension 0
- illumination: float32 [1088, 10, 1080], P('strip', 'batch'), parts along dimension 1
- mean_field: float32 [1088, 10, 1080], P('strip', 'batch'), parts along dimension 1
The draws below stay inside these ranges and needn't reach their ends.
There are 2 independent parts, one for each index of `batch`. The reference program is written for one: setup_inputs(seed, part) draws one part's arguments, and reference() takes and returns one part's arrays. A program takes and returns all parts, laid end to end along the dimension named above; an argument that names none is the same for every part. Nothing has to cross between parts.
Inputs may be any that keep to these rules, and one draw needn't show every extreme that they name: `fields`: positive intensities.
All inputs are finite; a program needn't handle non-finite values.
Results may differ from the reference program's by a relative error of at most 0.0004.
The reference program's roundings to bfloat16 on the way (of `illum_round`) count: a program that leaves them out, or rounds other values in their place, can miss the bound.
Values may be sent and summed in bfloat16 or wider, within the bound.
A program may use at most 192 MiB of HBM per device.

```python
import math
import jax
import jax.numpy as jnp
from jax import lax

C = 5
H = 1088
W = 1080
SIGMA = 16
RADIUS = 48
FIELDS = 16


def draw_fields(key, part):
    key_bright, key_texture = jax.random.split(key, 2)
    rows = jnp.arange(H, dtype=jnp.float32) / H - 0.5
    cols = jnp.arange(W, dtype=jnp.float32) / W - 0.5
    vignette = 0.4 + jnp.exp(-(rows[:, None, None] ** 2 + cols[None, None, :] ** 2) / 0.18)
    bright = jnp.exp(jax.random.uniform(key_bright, (FIELDS, 1, C, 1), jnp.float32, 0.0, math.log(10.0)))
    texture = jax.random.uniform(key_texture, (FIELDS, H, C, W), jnp.float32, 0.3, 3.0)
    return (bright * vignette[None] * texture).astype(jnp.bfloat16)


def setup_inputs(seed: int = 0, part: int = 0) -> dict:
    key_of = jax.random.split(jax.random.key(seed), 3)
    part_splits = jax.random.split(jax.random.fold_in(key_of[2], part), 3)
    return {
        "fields": draw_fields(jax.random.fold_in(jax.random.fold_in(key_of[2], part), 71), part),
        "flat_gain": jnp.clip(1.0 + 0.1 * jax.random.normal(key_of[1], (H, C, W), jnp.float32), 0.5, 1.5).astype(jnp.bfloat16),
    }


def kernel_table(length):
    index = jnp.arange(length, dtype=jnp.float32)
    offset = index[:, None] - index[None, :]
    weights = jnp.where(jnp.abs(offset) <= RADIUS, jnp.exp(-offset * offset / (2.0 * SIGMA * SIGMA)), 0.0)
    return weights / jnp.sum(weights, axis=1, keepdims=True)


def reference(fields, flat_gain):
    def accumulate(carry, field):
        return carry + field.astype(jnp.float32), None

    total, unused = lax.scan(accumulate, jnp.zeros((H, C, W), jnp.float32), fields)
    mean_field = total / FIELDS
    smooth_cols = jnp.einsum("hcv,wv->hcw", mean_field, kernel_table(W), precision=lax.Precision.HIGHEST)
    illumination = jnp.einsum("hu,ucw->hcw", kernel_table(H), smooth_cols, precision=lax.Precision.HIGHEST)
    illum_round = (illumination * flat_gain.astype(jnp.float32)).astype(jnp.bfloat16).astype(jnp.float32)

    def divide(field):
        return (field.astype(jnp.float32) / illum_round).astype(jnp.bfloat16)

    corrected = lax.map(divide, fields)
    return corrected, illumination, mean_field
```

```python
import functools
import jax
import jax.numpy as jnp
import numpy as np
from jax import lax
from jax.experimental import pallas as pl
from jax.experimental.pallas import tpu as pltpu
from jax.sharding import PartitionSpec as P

SIGMA = 16
RADIUS = 48
ROWS = 8
WIDE = 256
REACH = 512
LANES = 128
MESH = pl.DeviceIdType.MESH
LINK = jnp.bfloat16


def coded(mean):
    for _ in range(4):
        mean = mean * mean
    return mean.astype(LINK)


def decoded(code):
    code = code.astype(jnp.float32)
    for _ in range(4):
        code = lax.rsqrt(code)
    return code


def padded_2(array, sides, width):
    for axis, dim in sides:
        count, length = (lax.axis_size(axis), array.shape[dim])
        up = [(i, (i + 1) % count) for i in range(count - 1)]
        down = [(j, i) for i, j in up]
        last = lax.slice_in_dim(array, length - width, length, axis=dim)
        first = lax.slice_in_dim(array, 0, width, axis=dim)
        before = lax.ppermute(last, axis, up)
        after = lax.ppermute(first, axis, down)
        array = jnp.concatenate([before, array, after], axis=dim)
    return array


def gauss_weights(out_index, in_index, length):
    offset = out_index[:, None] - in_index[None, :]
    inside = (jnp.abs(offset) <= RADIUS) & (in_index[None, :] >= 0.0) & (in_index[None, :] < length)
    weights = jnp.where(inside, jnp.exp(-offset * offset / (2.0 * SIGMA * SIGMA)), 0.0)
    return weights / jnp.sum(weights, axis=1, keepdims=True)


def gauss_table(length):
    index = np.arange(length, dtype=np.float64)
    offset = index[:, None] - index[None, :]
    weights = np.where(np.abs(offset) <= RADIUS, np.exp(-offset * offset / (2.0 * SIGMA * SIGMA)), 0.0)
    return weights / np.sum(weights, axis=1, keepdims=True)


def halves(table):
    table = table.astype(np.float32)
    high = table.astype(jnp.bfloat16)
    low = (table - high.astype(np.float32)).astype(jnp.bfloat16)
    return np.stack([high, low])


def row_tables(height, strips):
    rows = height // strips
    gap = -rows % 16
    table = np.pad(gauss_table(height), ((0, 0), (RADIUS, RADIUS)))
    out = []
    for s in range(strips):
        own = table[s * rows:(s + 1) * rows]
        first = s * rows + RADIUS
        out.append(halves(np.concatenate([
            own[:, first:first + rows], np.zeros((rows, gap)),
            own[:, first - RADIUS:first], own[:, first + rows:first + rows + RADIUS]], axis=1)))
    return np.stack(out)


def column_tiles(width):
    padded = -(-width // LANES) * LANES
    table = np.pad(gauss_table(width).T, ((0, padded - width), (0, padded + WIDE - width)))
    tables, plan = [], []
    for w in range(0, padded, WIDE):
        start = min(max(w - LANES, 0), padded - REACH)
        block = halves(table[start:start + REACH, w:w + WIDE])
        same = [i for i, other in enumerate(tables) if np.array_equal(block, other)]
        if not same:
            tables.append(block)
        plan.append((w, min(WIDE, padded - w), min(WIDE, width - w), start, same[0] if same else len(tables) - 1))
    return np.stack(tables), plan


def split(value):
    high = value.astype(jnp.bfloat16)
    return high, (value - high.astype(jnp.float32)).astype(jnp.bfloat16)


def product(a, b):
    dot = functools.partial(jnp.dot, preferred_element_type=jnp.float32)
    return dot(a[0], b[0]) + (dot(a[0], b[1]) + dot(a[1], b[0]))


def at(strip, plate):
    return {"strip": strip, "plate": plate}


def spread_first(c):
    return lax.rem(c, 2) == 1


def fused_kernel(plan, x_ref, gain_ref, kh_ref, kw_ref, out_ref, illum_ref, mean_ref,
                 raw, turned, sib, ybuf, zbuf, mean, halo, gath, illum, gain, kh, kw, padded, rowed,
                 load_sem, again_sem, weight_sem, sib_send, sib_recv, y_send, y_recv, z_send, z_recv,
                 h_send, h_recv, m_send, m_recv, i_send, i_recv, mean_sem, illum_sem, out_sem, g_send, g_recv):
    channels, nz, _, rows, width = turned.shape
    strips = nz * 2
    strip, plate = lax.axis_index("strip"), lax.axis_index("plate")
    y, z = lax.rem(strip, 2), lax.div(strip, 2)
    owner = y == plate
    smoother = jnp.logical_not(owner)
    line = 1 - plate
    has_before, has_after = strip >= 1, strip + 1 < strips
    sibling, across = at(strip, 1 - plate), at(z * 2 + 1 - y, plate)
    diagonal = at(lax.rem(strip + 2 * y - 1 + strips, strips), plate)
    gap = padded.shape[1] - 2 * RADIUS

    def remote(src, dst, send, recv, target):
        return pltpu.make_async_remote_copy(src, dst, send, recv, device_id=target, device_id_type=MESH)

    def level(d):
        return lax.rem(z + d, nz)

    def load(c):
        return pltpu.make_async_copy(x_ref.at[c], raw.at[lax.rem(c, 2)], load_sem.at[c])

    def load_again(c):
        return pltpu.make_async_copy(x_ref.at[c], raw.at[lax.rem(c, 2)], again_sem.at[c])

    def store(c):
        return pltpu.make_async_copy(raw.at[lax.rem(c, 2)], out_ref.at[c], out_sem.at[c])

    def weights():
        return [pltpu.make_async_copy(gain_ref, gain, weight_sem.at[0]),
                pltpu.make_async_copy(kh_ref.at[strip], kh, weight_sem.at[1]),
                pltpu.make_async_copy(kw_ref, kw, weight_sem.at[2])]

    def to_sibling(c):
        return remote(turned.at[c, :, 1 - plate], sib.at[c], sib_send.at[c], sib_recv.at[c], sibling)

    def over(c, k):
        return remote(sib.at[c, k], ybuf.at[c, k], y_send.at[c, k], y_recv.at[c, k], across)

    def along(c, d):
        return remote(sib.at[c, level(d)], zbuf.at[c, d - 1], z_send.at[c, d - 1], z_recv.at[c, d - 1],
                      at(level(d) * 2 + y, plate))

    def halo_up(c):
        return remote(halo.at[c, 1], halo.at[c, 0], h_send.at[c, 1], h_recv.at[c, 0],
                      at(lax.rem(strip + 1, strips), plate))

    def halo_down(c):
        return remote(halo.at[c, 0], halo.at[c, 1], h_send.at[c, 0], h_recv.at[c, 1],
                      at(lax.rem(strip + strips - 1, strips), plate))

    def share_mean(c):
        return remote(mean.at[c], mean.at[c], m_send.at[c], m_recv.at[c], sibling)

    def store_mean(c):
        return pltpu.make_async_copy(mean.at[c], mean_ref.at[c], mean_sem.at[c])

    def store_illum(c):
        return pltpu.make_async_copy(illum.at[lax.rem(c, 2)], illum_ref.at[c], illum_sem.at[c])

    def share_illum(c):
        return remote(illum.at[lax.rem(c, 2)], illum_ref.at[c], i_send.at[c], i_recv.at[c], sibling)

    def gather(c, k, kind):
        target = (sibling, across, at(lax.rem(strip + 2, strips), plate),
                  at(lax.rem(strip + strips - 2, strips), plate))[kind]
        slot = gath.at[c, k, line]
        return remote(slot, slot, g_send.at[c, k, kind], g_recv.at[c, k, line], target)

    def gathered(c, k):
        slot = gath.at[c, k, plate]
        return remote(slot, slot, g_send.at[c, k, 0], g_recv.at[c, k, plate], sibling)

    def turn(c):
        load(c).wait()
        for w in range(0, width, WIDE):
            wide = min(WIDE, width - w)
            block = jnp.transpose(raw[lax.rem(c, 2), pl.ds(w, wide), :])
            for k in range(strips):
                turned[c, k // 2, k % 2, :, pl.ds(w, wide)] = block[k * rows:(k + 1) * rows]
        pl.when(c + 2 < channels)(lambda: load(c + 2).start())

    def paired(c, k, r):
        at_r = pl.ds(r, ROWS)
        return turned[c, k, plate, at_r, :].astype(jnp.float32) + sib[c, k, at_r, :].astype(jnp.float32)

    def encode(c):
        to_sibling(c).wait_recv()

        @pl.loop(1, nz + 1)
        def _(d):
            k = level(d)
            for r in range(0, rows, ROWS):
                sib[c, k, pl.ds(r, ROWS), :] = coded(paired(c, k, r) * 0.5)
            over(c, k).start()

    def summed(c, k, r):
        return paired(c, k, r) + 2.0 * decoded(ybuf[c, k, pl.ds(r, ROWS), :])

    def across_sums(c):
        to_sibling(c).wait_recv()

        @pl.loop(1, nz)
        def _(d):
            k = level(d)
            over(c, k).wait_recv()
            for r in range(0, rows, ROWS):
                sib[c, k, pl.ds(r, ROWS), :] = coded(summed(c, k, r) * 0.25)
            along(c, d).start()

        over(c, z).wait_recv()
        for r in range(0, rows, ROWS):
            mean[c, pl.ds(r, ROWS), :] = summed(c, z, r)

    def finish_mean(c):
        @pl.loop(1, nz)
        def _(d):
            along(c, d).wait_recv()

        for r in range(0, rows, ROWS):
            at_r = pl.ds(r, ROWS)
            value = mean[c, at_r, :]
            for d in range(1, nz):
                value = value + 4.0 * decoded(zbuf[c, d - 1, at_r, :])
            value = value * (1.0 / (2 * strips))
            mean[c, at_r, :] = value
            if r < RADIUS:
                halo[c, 0, at_r, :] = coded(value)
            if r >= rows - RADIUS:
                halo[c, 1, pl.ds(r - rows + RADIUS, ROWS), :] = coded(value)
        pl.when(has_after)(lambda: halo_up(c).start())
        pl.when(has_before)(lambda: halo_down(c).start())
        share_mean(c).start()
        store_mean(c).start()

    def fill(r, value):
        at_r = pl.ds(r, value.shape[0])
        high, low = split(value)
        padded[0, at_r, pl.ds(0, width)] = high
        padded[1, at_r, pl.ds(0, width)] = low

    def smooth(c):
        share_mean(c).wait_recv()
        store_mean(c).start()
        for r in range(0, rows, ROWS):
            fill(r, mean[c, pl.ds(r, ROWS), :])

        @pl.when(has_before)
        def _():
            halo_up(c).wait_recv()
            for r in range(0, RADIUS, ROWS):
                fill(gap + r, decoded(halo[c, 0, pl.ds(r, ROWS), :]))

        @pl.when(has_after)
        def _():
            halo_down(c).wait_recv()
            for r in range(0, RADIUS, ROWS):
                fill(gap + RADIUS + r, decoded(halo[c, 1, pl.ds(r, ROWS), :]))

        for w, wide, _, _, _ in plan:
            cols = pl.ds(w, wide)
            value = product((kh[0], kh[1]), (padded[0, :, cols], padded[1, :, cols]))
            rowed[0, :, cols], rowed[1, :, cols] = split(value)

        @pl.when(c >= 2)
        def _():
            store_illum(c - 2).wait()
            share_illum(c - 2).wait_send()

        for w, wide, used, start, index in plan:
            reach = pl.ds(start, REACH)
            value = product((rowed[0, :, reach], rowed[1, :, reach]),
                            (kw[index, 0, :, pl.ds(0, wide)], kw[index, 1, :, pl.ds(0, wide)]))[:, :used]
            cols = pl.ds(w, used)
            illum[lax.rem(c, 2), :, cols] = value
            gath[c, z, y, :, cols] = (value * gain[c, :, cols].astype(jnp.float32)).astype(jnp.bfloat16)
        pl.when(z + 1 < nz)(lambda: gather(c, z, 2).start())
        pl.when(z >= 1)(lambda: gather(c, z, 3).start())
        gather(c, z, 1).start()
        gather(c, z, 0).start()
        store_illum(c).start()
        share_illum(c).start()

    def relay(c):
        lined = smoother | spread_first(c)
        crossing = smoother & jnp.logical_not(spread_first(c))

        @pl.loop(0, nz)
        def _(d):
            @pl.when((z - d >= 0) & ((d > 0) | owner))
            def _():
                k = z - d
                gather(c, k, 0).wait_recv()
                pl.when(lined & (z + 1 < nz))(lambda: gather(c, k, 2).start())
                pl.when(lined & (d == 0) & (z >= 1))(lambda: gather(c, k, 3).start())
                pl.when(crossing)(lambda: gather(c, k, 1).start())
                gather(c, k, 0).start()

            @pl.when((z + d < nz) & (d > 0))
            def _():
                k = z + d
                gather(c, k, 0).wait_recv()
                pl.when(lined & (z >= 1))(lambda: gather(c, k, 3).start())
                pl.when(crossing)(lambda: gather(c, k, 1).start())
                gather(c, k, 0).start()

    def divide(c):
        @pl.loop(0, nz)
        def _(k):
            gathered(c, k).wait_recv()

        load_again(c).wait()
        slot = lax.rem(c, 2)

        def part(w, wide):
            block = gath[c, :, :, :, pl.ds(w, wide)].reshape(strips * rows, wide)
            below = jnp.transpose(block).astype(jnp.float32)
            value = raw[slot, pl.ds(w, wide), :].astype(jnp.float32) / below
            raw[slot, pl.ds(w, wide), :] = value.astype(raw.dtype)

        full = width // LANES

        @pl.loop(0, full)
        def _(i):
            part(pl.multiple_of(i * LANES, LANES), LANES)

        if width % LANES:
            part(full * LANES, width % LANES)
        store(c).start()

        @pl.when((c >= 1) & (c + 1 < channels))
        def _():
            store(c - 1).wait()
            load_again(c + 1).start()

    partners = [sibling, across, diagonal] + [at(level(d) * 2 + y, plate) for d in range(1, nz)]
    load(0).start()
    load(1).start()
    for copy in weights():
        copy.start()
    barrier = pltpu.get_barrier_semaphore()
    for partner in partners:
        pl.semaphore_signal(barrier, inc=1, device_id=partner, device_id_type=MESH)
    pl.semaphore_wait(barrier, len(partners))

    def turn_and_send(c):
        turn(c)
        to_sibling(c).start()

    @pl.when(smoother)
    def _():
        padded[...] = jnp.zeros_like(padded)

        @pl.loop(0, channels + 1)
        def _(c):
            pl.when(c < channels)(lambda: turn_and_send(c))
            pl.when(c >= 1)(lambda: encode(c - 1))

        load_again(0).start()
        load_again(1).start()
        for copy in weights():
            copy.wait()

        @pl.loop(0, channels + 2)
        def _(c):
            pl.when(c < channels)(lambda: smooth(c))
            pl.when((c >= 1) & (c <= channels))(lambda: relay(c - 1))
            pl.when(c >= 2)(lambda: divide(c - 2))

    @pl.when(owner)
    def _():
        turn_and_send(0)
        turn_and_send(1)

        @pl.loop(0, channels * 2)
        def _(c):
            pl.when(c == 0)(lambda: turn_and_send(2))

            @pl.when(c < channels)
            def _():
                across_sums(c)

            @pl.when(c == 0)
            def _():
                turn_and_send(3)
                turn_and_send(4)
                load_again(0).start()
                load_again(1).start()

            pl.when((c >= 1) & (c <= channels))(lambda: finish_mean(c - 1))
            pl.when((c >= 4) & (c < channels + 4))(lambda: relay(c - 4))
            pl.when(c >= 5)(lambda: divide(c - 5))

        for copy in weights():
            copy.wait()

        @pl.loop(0, channels)
        def _(c):
            share_illum(c).wait_recv()

    @pl.loop(0, channels)
    def _(c):
        to_sibling(c).wait_send()
        store_mean(c).wait()
        pl.when(c >= channels - 2)(lambda: store(c).wait())

        @pl.when(smoother)
        def _():
            @pl.when(c >= channels - 2)
            def _():
                store_illum(c).wait()
                share_illum(c).wait_send()

            @pl.loop(0, nz)
            def _(k):
                over(c, k).wait_send()

        @pl.when(owner)
        def _():
            share_mean(c).wait_send()
            pl.when(has_after)(lambda: halo_up(c).wait_send())
            pl.when(has_before)(lambda: halo_down(c).wait_send())

            @pl.loop(1, nz)
            def _(d):
                along(c, d).wait_send()

        lined = smoother | spread_first(c)

        @pl.loop(0, nz)
        def _(k):
            gather(c, k, 0).wait_send()
            crossed = smoother & ((k == z) | jnp.logical_not(spread_first(c)))
            pl.when(crossed)(lambda: gather(c, k, 1).wait_send())
            pl.when(lined & (k <= z) & (z + 1 < nz))(lambda: gather(c, k, 2).wait_send())
            pl.when(lined & (k >= z) & (z >= 1))(lambda: gather(c, k, 3).wait_send())


def fused(x, gain, strips):
    channels, width, height = x.shape
    rows, nz = height // strips, strips // 2
    padded_width = -(-width // LANES) * LANES
    kh = row_tables(height, strips)
    kw, plan = column_tiles(width)
    dma = pltpu.SemaphoreType.DMA
    each, levels = dma((channels,)), dma((channels, nz))
    part = (channels, nz, rows, width)
    own = (channels, rows, width)
    anywhere = pl.BlockSpec(memory_space=pl.ANY)
    return pl.pallas_call(
        functools.partial(fused_kernel, plan),
        out_shape=[jax.ShapeDtypeStruct(x.shape, x.dtype), jax.ShapeDtypeStruct(own, jnp.float32),
                   jax.ShapeDtypeStruct(own, jnp.float32)],
        in_specs=[anywhere] * 4,
        out_specs=[anywhere] * 3,
        scratch_shapes=[
            pltpu.VMEM((2, width, height), x.dtype),
            pltpu.VMEM((channels, nz, 2, rows, width), x.dtype),
            pltpu.VMEM(part, LINK),
            pltpu.VMEM(part, LINK),
            pltpu.VMEM((channels, nz - 1, rows, width), LINK),
            pltpu.VMEM(own, jnp.float32),
            pltpu.VMEM((channels, 2, RADIUS, width), LINK),
            pltpu.VMEM((channels, nz, 2, rows, width), jnp.bfloat16),
            pltpu.VMEM((2, rows, width), jnp.float32),
            pltpu.VMEM(own, gain.dtype),
            pltpu.VMEM(kh.shape[1:], jnp.bfloat16),
            pltpu.VMEM(kw.shape, jnp.bfloat16),
            pltpu.VMEM((2, kh.shape[3], padded_width), jnp.bfloat16),
            pltpu.VMEM((2, rows, padded_width), jnp.bfloat16),
            each, each, dma((3,)), each, each, levels, levels, levels, levels,
            dma((channels, 2)), dma((channels, 2)), each, each, each, each, each, each, each,
            dma((channels, nz, 4)), dma((channels, nz, 2)),
        ],
        compiler_params=pltpu.CompilerParams(
            collective_id=0, has_side_effects=True, vmem_limit_bytes=60 * 2**20),
        name="fused",
    )(x, gain, kh, kw)


def on_grid(fields, flat_gain):
    x = jnp.transpose(fields[0], (1, 2, 0))
    gain = jnp.transpose(flat_gain, (1, 0, 2))
    corrected, illumination, mean_field = fused(x, gain, lax.axis_size("strip"))
    back = lambda a: jnp.transpose(a, (1, 0, 2))
    return (jnp.transpose(corrected, (2, 0, 1))[None], back(illumination), back(mean_field))


def on_device(fields, flat_gain):
    num_fields, height, channels, width = fields.shape
    strips = lax.axis_size("strip")
    plates = lax.axis_size("plate")
    strip_rows = height // strips
    count = num_fields * strips * plates
    block = fields
    partial_sum = lax.psum_scatter(
        jnp.sum(block, axis=0, dtype=jnp.float32), "strip", scatter_dimension=0, tiled=True
    )
    total = lax.psum(partial_sum, "plate")
    mean_field = total / count
    col_index = jnp.arange(width, dtype=jnp.float32)
    col_kernel = gauss_weights(col_index, col_index, float(width))
    smooth_cols = jnp.einsum("hcv,wv->hcw", mean_field, col_kernel, precision=lax.Precision.HIGHEST)
    padded = padded_2(smooth_cols, (("strip", 0),), RADIUS)
    first_row = (lax.axis_index("strip") * strip_rows).astype(jnp.float32)
    out_index = first_row + jnp.arange(strip_rows, dtype=jnp.float32)
    in_index = first_row - RADIUS + jnp.arange(strip_rows + 2 * RADIUS, dtype=jnp.float32)
    row_kernel = gauss_weights(out_index, in_index, float(height))
    illumination = jnp.einsum("hu,ucw->hcw", row_kernel, padded, precision=lax.Precision.HIGHEST)
    illum_round = (illumination * flat_gain.astype(jnp.float32)).astype(jnp.bfloat16)
    block = fields
    corrected = (
        block.astype(jnp.float32)
        / lax.all_gather(illum_round, "strip", axis=0, tiled=True).astype(jnp.float32)[None]
    ).astype(jnp.bfloat16)
    return (corrected, illumination, mean_field)


def solution(mesh):
    grid = mesh.shape["strip"] == 8 and mesh.shape["plate"] == 2
    return jax.shard_map(
        on_grid if grid else on_device,
        mesh=mesh,
        in_specs=(P(("batch", "strip", "plate"), None, None, None), P("strip", None, None)),
        out_specs=(
            P(("batch", "strip", "plate"), None, None, None),
            P("strip", "batch", None),
            P("strip", "batch", None),
        ),
        check_vma=False,
    )
```

```python
import functools
import jax
import jax.numpy as jnp
import numpy as np
from jax import lax
from jax.experimental import pallas as pl
from jax.experimental.pallas import tpu as pltpu
from jax.sharding import PartitionSpec as P

SIGMA = 16
RADIUS = 48
ROWS = 8
WIDE = 256
REACH = 512
LANES = 128
MESH = pl.DeviceIdType.MESH
LINK = jnp.bfloat16


def coded(mean):
    for _ in range(4):
        mean = mean * mean
    return mean.astype(LINK)


def decoded(code):
    code = code.astype(jnp.float32)
    for _ in range(4):
        code = lax.rsqrt(code)
    return code


def padded_2(array, sides, width):
    for axis, dim in sides:
        count, length = (lax.axis_size(axis), array.shape[dim])
        up = [(i, (i + 1) % count) for i in range(count - 1)]
        down = [(j, i) for i, j in up]
        last = lax.slice_in_dim(array, length - width, length, axis=dim)
        first = lax.slice_in_dim(array, 0, width, axis=dim)
        before = lax.ppermute(last, axis, up)
        after = lax.ppermute(first, axis, down)
        array = jnp.concatenate([before, array, after], axis=dim)
    return array


def gauss_weights(out_index, in_index, length):
    offset = out_index[:, None] - in_index[None, :]
    inside = (jnp.abs(offset) <= RADIUS) & (in_index[None, :] >= 0.0) & (in_index[None, :] < length)
    weights = jnp.where(inside, jnp.exp(-offset * offset / (2.0 * SIGMA * SIGMA)), 0.0)
    return weights / jnp.sum(weights, axis=1, keepdims=True)


def gauss_table(length):
    index = np.arange(length, dtype=np.float64)
    offset = index[:, None] - index[None, :]
    weights = np.where(np.abs(offset) <= RADIUS, np.exp(-offset * offset / (2.0 * SIGMA * SIGMA)), 0.0)
    return weights / np.sum(weights, axis=1, keepdims=True)


def halves(table):
    table = table.astype(np.float32)
    high = table.astype(jnp.bfloat16)
    low = (table - high.astype(np.float32)).astype(jnp.bfloat16)
    return np.stack([high, low])


def row_tables(height, strips):
    rows = height // strips
    gap = -rows % 16
    table = np.pad(gauss_table(height), ((0, 0), (RADIUS, RADIUS)))
    out = []
    for s in range(strips):
        own = table[s * rows:(s + 1) * rows]
        first = s * rows + RADIUS
        out.append(halves(np.concatenate([
            own[:, first:first + rows], np.zeros((rows, gap)),
            own[:, first - RADIUS:first], own[:, first + rows:first + rows + RADIUS]], axis=1)))
    return np.stack(out)


def column_tiles(width):
    padded = -(-width // LANES) * LANES
    table = np.pad(gauss_table(width).T, ((0, padded - width), (0, padded + WIDE - width)))
    tables, plan = [], []
    for w in range(0, padded, WIDE):
        start = min(max(w - LANES, 0), padded - REACH)
        block = halves(table[start:start + REACH, w:w + WIDE])
        same = [i for i, other in enumerate(tables) if np.array_equal(block, other)]
        if not same:
            tables.append(block)
        plan.append((w, min(WIDE, padded - w), min(WIDE, width - w), start, same[0] if same else len(tables) - 1))
    return np.stack(tables), plan


def split(value):
    high = value.astype(jnp.bfloat16)
    return high, (value - high.astype(jnp.float32)).astype(jnp.bfloat16)


def product(a, b):
    dot = functools.partial(jnp.dot, preferred_element_type=jnp.float32)
    return dot(a[0], b[0]) + (dot(a[0], b[1]) + dot(a[1], b[0]))


def at(strip, plate):
    return {"strip": strip, "plate": plate}


def spread_first(c):
    return c < 0


def fused_kernel(plan, x_ref, gain_ref, kh_ref, kw_ref, out_ref, illum_ref, mean_ref,
                 turned, sib, ybuf, zbuf, halo, gain, kh, kw, padded, rowed,
                 load_sem, weight_sem, freed, sib_send, sib_recv, y_send, y_recv, z_send, z_recv,
                 h_send, h_recv, m_send, m_recv, i_send, i_recv, g_send, g_recv):
    channels, nz, _, rows, width = turned.shape
    strips = nz * 2
    strip, plate = lax.axis_index("strip"), lax.axis_index("plate")
    y, z = lax.rem(strip, 2), lax.div(strip, 2)
    owner = y == plate
    smoother = jnp.logical_not(owner)
    line = 1 - plate
    has_before, has_after = strip >= 1, strip + 1 < strips
    sibling, across = at(strip, 1 - plate), at(z * 2 + 1 - y, plate)
    diagonal = at(lax.rem(strip + 2 * y - 1 + strips, strips), plate)
    gap = padded.shape[1] - 2 * RADIUS

    def remote(src, dst, send, recv, target):
        return pltpu.make_async_remote_copy(src, dst, send, recv, device_id=target, device_id_type=MESH)

    def level(d):
        return lax.rem(z + d, nz)

    def load(c):
        return pltpu.make_async_copy(x_ref.at[c], out_ref.at[c], load_sem.at[c])

    def weights():
        return [pltpu.make_async_copy(gain_ref, gain, weight_sem.at[0]),
                pltpu.make_async_copy(kh_ref.at[strip], kh, weight_sem.at[1]),
                pltpu.make_async_copy(kw_ref, kw, weight_sem.at[2])]

    def to_sibling(c):
        return remote(turned.at[c, :, 1 - plate], sib.at[c], sib_send.at[c], sib_recv.at[c], sibling)

    def over(c, k):
        return remote(sib.at[c, k], ybuf.at[c, k], y_send.at[c, k], y_recv.at[c, k], across)

    def along(c, d):
        return remote(sib.at[c, level(d)], zbuf.at[c, d - 1], z_send.at[c, d - 1], z_recv.at[c, d - 1],
                      at(level(d) * 2 + y, plate))

    def halo_up(c):
        return remote(halo.at[c, 1], halo.at[c, 0], h_send.at[c, 1], h_recv.at[c, 0],
                      at(lax.rem(strip + 1, strips), plate))

    def halo_down(c):
        return remote(halo.at[c, 0], halo.at[c, 1], h_send.at[c, 0], h_recv.at[c, 1],
                      at(lax.rem(strip + strips - 1, strips), plate))

    def share_mean(c):
        return remote(mean_ref.at[c], mean_ref.at[c], m_send.at[c], m_recv.at[c], sibling)

    def share_illum(c):
        return remote(illum_ref.at[c], illum_ref.at[c], i_send.at[c], i_recv.at[c], sibling)

    def gather(c, k, kind):
        target = (sibling, across, at(lax.rem(strip + 2, strips), plate),
                  at(lax.rem(strip + strips - 2, strips), plate))[kind]
        slot = turned.at[c, k, line]
        return remote(slot, slot, g_send.at[c, k, kind], g_recv.at[c, k, line], target)

    def gathered(c, k):
        slot = turned.at[c, k, plate]
        return remote(slot, slot, g_send.at[c, k, 0], g_recv.at[c, k, plate], sibling)

    def turn(c):
        load(c).wait()
        for w in range(0, width, WIDE):
            wide = min(WIDE, width - w)
            block = jnp.transpose(out_ref[c, pl.ds(w, wide), :])
            for k in range(strips):
                turned[c, k // 2, k % 2, :, pl.ds(w, wide)] = block[k * rows:(k + 1) * rows]

    def paired(c, k, r):
        at_r = pl.ds(r, ROWS)
        return turned[c, k, plate, at_r, :].astype(jnp.float32) + sib[c, k, at_r, :].astype(jnp.float32)

    def release(c):
        to_sibling(c).wait_send()
        pl.semaphore_signal(freed.at[c], inc=1, device_id=sibling, device_id_type=MESH)

    def encode(c):
        to_sibling(c).wait_recv()
        release(c)

        @pl.loop(1, nz + 1)
        def _(d):
            k = level(d)
            for r in range(0, rows, ROWS):
                sib[c, k, pl.ds(r, ROWS), :] = coded(paired(c, k, r) * 0.5)
            pl.when(d == 1)(lambda: pl.semaphore_wait(freed.at[c], 1))
            over(c, k).start()

    def summed(c, k, r):
        return paired(c, k, r) + 2.0 * decoded(ybuf[c, k, pl.ds(r, ROWS), :])

    def across_sums(c):
        to_sibling(c).wait_recv()
        pl.semaphore_wait(freed.at[c], 1)

        @pl.loop(1, nz)
        def _(d):
            k = level(d)
            over(c, k).wait_recv()
            for r in range(0, rows, ROWS):
                sib[c, k, pl.ds(r, ROWS), :] = coded(summed(c, k, r) * 0.25)
            along(c, d).start()

        over(c, z).wait_recv()
        for r in range(0, rows, ROWS):
            mean_ref[c, pl.ds(r, ROWS), :] = summed(c, z, r)

    def finish_mean(c):
        @pl.loop(1, nz)
        def _(d):
            along(c, d).wait_recv()

        for r in range(0, rows, ROWS):
            at_r = pl.ds(r, ROWS)
            value = mean_ref[c, at_r, :]
            for d in range(1, nz):
                value = value + 4.0 * decoded(zbuf[c, d - 1, at_r, :])
            value = value * (1.0 / (2 * strips))
            mean_ref[c, at_r, :] = value
            if r < RADIUS:
                halo[c, 0, at_r, :] = coded(value)
            if r >= rows - RADIUS:
                halo[c, 1, pl.ds(r - rows + RADIUS, ROWS), :] = coded(value)
        pl.when(has_after)(lambda: halo_up(c).start())
        pl.when(has_before)(lambda: halo_down(c).start())
        share_mean(c).start()

    def fill(r, value):
        at_r = pl.ds(r, value.shape[0])
        high, low = split(value)
        padded[0, at_r, pl.ds(0, width)] = high
        padded[1, at_r, pl.ds(0, width)] = low

    def smooth(c):
        share_mean(c).wait_recv()
        for r in range(0, rows, ROWS):
            fill(r, mean_ref[c, pl.ds(r, ROWS), :])

        @pl.when(has_before)
        def _():
            halo_up(c).wait_recv()
            for r in range(0, RADIUS, ROWS):
                fill(gap + r, decoded(halo[c, 0, pl.ds(r, ROWS), :]))

        @pl.when(has_after)
        def _():
            halo_down(c).wait_recv()
            for r in range(0, RADIUS, ROWS):
                fill(gap + RADIUS + r, decoded(halo[c, 1, pl.ds(r, ROWS), :]))

        for w, wide, _, _, _ in plan:
            cols = pl.ds(w, wide)
            value = product((kh[0], kh[1]), (padded[0, :, cols], padded[1, :, cols]))
            rowed[0, :, cols], rowed[1, :, cols] = split(value)

        for w, wide, used, start, index in plan:
            reach = pl.ds(start, REACH)
            value = product((rowed[0, :, reach], rowed[1, :, reach]),
                            (kw[index, 0, :, pl.ds(0, wide)], kw[index, 1, :, pl.ds(0, wide)]))[:, :used]
            cols = pl.ds(w, used)
            illum_ref[c, :, cols] = value
            turned[c, z, y, :, cols] = (value * gain[c, :, cols].astype(jnp.float32)).astype(jnp.bfloat16)
        pl.when(z + 1 < nz)(lambda: gather(c, z, 2).start())
        pl.when(z >= 1)(lambda: gather(c, z, 3).start())
        gather(c, z, 1).start()
        gather(c, z, 0).start()
        share_illum(c).start()

    def relay(c):
        lined = smoother | spread_first(c)
        crossing = smoother & jnp.logical_not(spread_first(c))

        @pl.loop(0, nz)
        def _(d):
            @pl.when((z - d >= 0) & ((d > 0) | owner))
            def _():
                k = z - d
                gather(c, k, 0).wait_recv()
                pl.when(lined & (z + 1 < nz))(lambda: gather(c, k, 2).start())
                pl.when(lined & (d == 0) & (z >= 1))(lambda: gather(c, k, 3).start())
                pl.when(crossing)(lambda: gather(c, k, 1).start())
                gather(c, k, 0).start()

            @pl.when((z + d < nz) & (d > 0))
            def _():
                k = z + d
                gather(c, k, 0).wait_recv()
                pl.when(lined & (z >= 1))(lambda: gather(c, k, 3).start())
                pl.when(crossing)(lambda: gather(c, k, 1).start())
                gather(c, k, 0).start()

    def divide(c):
        @pl.loop(0, nz)
        def _(k):
            gathered(c, k).wait_recv()

        def part(w, wide):
            block = turned[c, :, :, :, pl.ds(w, wide)].reshape(strips * rows, wide)
            below = jnp.transpose(block).astype(jnp.float32)
            value = out_ref[c, pl.ds(w, wide), :].astype(jnp.float32) / below
            out_ref[c, pl.ds(w, wide), :] = value.astype(out_ref.dtype)

        full = width // LANES

        @pl.loop(0, full)
        def _(i):
            part(pl.multiple_of(i * LANES, LANES), LANES)

        if width % LANES:
            part(full * LANES, width % LANES)

    partners = [sibling, across, diagonal] + [at(level(d) * 2 + y, plate) for d in range(1, nz)]
    load(0).start()
    barrier = pltpu.get_barrier_semaphore()
    for partner in partners:
        pl.semaphore_signal(barrier, inc=1, device_id=partner, device_id_type=MESH)
    load(1).start()
    turn(0)
    pl.semaphore_wait(barrier, len(partners))
    to_sibling(0).start()
    for c in range(2, channels):
        load(c).start()
    for copy in weights():
        copy.start()

    def turn_and_send(c):
        turn(c)
        to_sibling(c).start()

    @pl.when(smoother)
    def _():
        padded[...] = jnp.zeros_like(padded)

        @pl.loop(1, channels + 1)
        def _(c):
            pl.when(c < channels)(lambda: turn_and_send(c))
            encode(c - 1)

        for copy in weights():
            copy.wait()

        @pl.loop(0, channels + 2)
        def _(c):
            pl.when(c < channels)(lambda: smooth(c))
            pl.when((c >= 1) & (c <= channels))(lambda: relay(c - 1))
            pl.when(c >= 2)(lambda: divide(c - 2))

    @pl.when(owner)
    def _():
        @pl.loop(1, channels + 1)
        def _(c):
            pl.when(c < channels)(lambda: turn_and_send(c))
            release(c - 1)

        @pl.loop(0, channels * 2)
        def _(c):
            pl.when(c < channels)(lambda: across_sums(c))
            pl.when((c >= 1) & (c <= channels))(lambda: finish_mean(c - 1))
            pl.when((c >= 4) & (c < channels + 4))(lambda: relay(c - 4))
            pl.when(c >= 5)(lambda: divide(c - 5))

        for copy in weights():
            copy.wait()

        @pl.loop(0, channels)
        def _(c):
            share_illum(c).wait_recv()

    @pl.loop(0, channels)
    def _(c):
        @pl.when(smoother)
        def _():
            share_illum(c).wait_send()

            @pl.loop(0, nz)
            def _(k):
                over(c, k).wait_send()

        @pl.when(owner)
        def _():
            share_mean(c).wait_send()
            pl.when(has_after)(lambda: halo_up(c).wait_send())
            pl.when(has_before)(lambda: halo_down(c).wait_send())

            @pl.loop(1, nz)
            def _(d):
                along(c, d).wait_send()

        lined = smoother | spread_first(c)

        @pl.loop(0, nz)
        def _(k):
            gather(c, k, 0).wait_send()
            crossed = smoother & ((k == z) | jnp.logical_not(spread_first(c)))
            pl.when(crossed)(lambda: gather(c, k, 1).wait_send())
            pl.when(lined & (k <= z) & (z + 1 < nz))(lambda: gather(c, k, 2).wait_send())
            pl.when(lined & (k >= z) & (z >= 1))(lambda: gather(c, k, 3).wait_send())


def fused(x, gain, strips):
    channels, width, height = x.shape
    rows, nz = height // strips, strips // 2
    padded_width = -(-width // LANES) * LANES
    kh = row_tables(height, strips)
    kw, plan = column_tiles(width)
    dma = pltpu.SemaphoreType.DMA
    each, levels = dma((channels,)), dma((channels, nz))
    part = (channels, nz, rows, width)
    own = (channels, rows, width)
    anywhere = pl.BlockSpec(memory_space=pl.ANY)
    held = [pltpu.VMEM(x.shape, x.dtype), pltpu.VMEM(own, jnp.float32), pltpu.VMEM(own, jnp.float32)]
    return pl.pallas_call(
        functools.partial(fused_kernel, plan),
        out_shape=held,
        in_specs=[anywhere] * 4,
        out_specs=[pl.BlockSpec(memory_space=pltpu.VMEM)] * 3,
        scratch_shapes=[
            pltpu.VMEM((channels, nz, 2, rows, width), x.dtype),
            pltpu.VMEM(part, LINK),
            pltpu.VMEM(part, LINK),
            pltpu.VMEM((channels, nz - 1, rows, width), LINK),
            pltpu.VMEM((channels, 2, RADIUS, width), LINK),
            pltpu.VMEM(own, gain.dtype),
            pltpu.VMEM(kh.shape[1:], jnp.bfloat16),
            pltpu.VMEM(kw.shape, jnp.bfloat16),
            pltpu.VMEM((2, kh.shape[3], padded_width), jnp.bfloat16),
            pltpu.VMEM((2, rows, padded_width), jnp.bfloat16),
            each, dma((3,)), pltpu.SemaphoreType.REGULAR((channels,)), each, each, levels, levels, levels, levels,
            dma((channels, 2)), dma((channels, 2)), each, each, each, each,
            dma((channels, nz, 4)), dma((channels, nz, 2)),
        ],
        compiler_params=pltpu.CompilerParams(
            collective_id=0, has_side_effects=True, vmem_limit_bytes=44 * 2**20),
        name="fused",
    )(x, gain, kh, kw)


def stored_kernel(*refs):
    sources, targets, sems = refs[:3], refs[3:6], refs[6]
    copies = [pltpu.make_async_copy(source.at[c], target.at[c], sems.at[i, c])
              for i, (source, target) in enumerate(zip(sources, targets)) for c in range(source.shape[0])]
    for copy in copies:
        copy.start()
    for copy in copies:
        copy.wait()


def stored(arrays):
    anywhere = pl.BlockSpec(memory_space=pl.ANY)
    return pl.pallas_call(
        stored_kernel,
        out_shape=[jax.ShapeDtypeStruct(a.shape, a.dtype) for a in arrays],
        in_specs=[pl.BlockSpec(memory_space=pltpu.VMEM)] * 3,
        out_specs=[anywhere] * 3,
        scratch_shapes=[pltpu.SemaphoreType.DMA((3, arrays[0].shape[0]))],
        compiler_params=pltpu.CompilerParams(vmem_limit_bytes=2**20),
        name="stored",
    )(*arrays)


def on_grid(fields, flat_gain):
    x = jnp.transpose(fields[0], (1, 2, 0))
    gain = jnp.transpose(flat_gain, (1, 0, 2))
    corrected, illumination, mean_field = stored(fused(x, gain, lax.axis_size("strip")))
    back = lambda a: jnp.transpose(a, (1, 0, 2))
    return (jnp.transpose(corrected, (2, 0, 1))[None], back(illumination), back(mean_field))


def on_device(fields, flat_gain):
    num_fields, height, channels, width = fields.shape
    strips = lax.axis_size("strip")
    plates = lax.axis_size("plate")
    strip_rows = height // strips
    count = num_fields * strips * plates
    block = fields
    partial_sum = lax.psum_scatter(
        jnp.sum(block, axis=0, dtype=jnp.float32), "strip", scatter_dimension=0, tiled=True
    )
    total = lax.psum(partial_sum, "plate")
    mean_field = total / count
    col_index = jnp.arange(width, dtype=jnp.float32)
    col_kernel = gauss_weights(col_index, col_index, float(width))
    smooth_cols = jnp.einsum("hcv,wv->hcw", mean_field, col_kernel, precision=lax.Precision.HIGHEST)
    padded = padded_2(smooth_cols, (("strip", 0),), RADIUS)
    first_row = (lax.axis_index("strip") * strip_rows).astype(jnp.float32)
    out_index = first_row + jnp.arange(strip_rows, dtype=jnp.float32)
    in_index = first_row - RADIUS + jnp.arange(strip_rows + 2 * RADIUS, dtype=jnp.float32)
    row_kernel = gauss_weights(out_index, in_index, float(height))
    illumination = jnp.einsum("hu,ucw->hcw", row_kernel, padded, precision=lax.Precision.HIGHEST)
    illum_round = (illumination * flat_gain.astype(jnp.float32)).astype(jnp.bfloat16)
    block = fields
    corrected = (
        block.astype(jnp.float32)
        / lax.all_gather(illum_round, "strip", axis=0, tiled=True).astype(jnp.float32)[None]
    ).astype(jnp.bfloat16)
    return (corrected, illumination, mean_field)


def solution(mesh):
    grid = mesh.shape["strip"] == 8 and mesh.shape["plate"] == 2
    return jax.shard_map(
        on_grid if grid else on_device,
        mesh=mesh,
        in_specs=(P(("batch", "strip", "plate"), None, None, None), P("strip", None, None)),
        out_specs=(
            P(("batch", "strip", "plate"), None, None, None),
            P("strip", "batch", None),
            P("strip", "batch", None),
        ),
        check_vma=False,
    )
```

```python
import functools
import jax
import jax.numpy as jnp
import numpy as np
from jax import lax
from jax.experimental import pallas as pl
from jax.experimental.pallas import tpu as pltpu
from jax.sharding import PartitionSpec as P

SIGMA = 16
RADIUS = 48
ROWS = 8
WIDE = 256
REACH = 512
LANES = 128
MESH = pl.DeviceIdType.MESH
LINK = jnp.bfloat16


def coded(mean):
    for _ in range(4):
        mean = mean * mean
    return mean.astype(LINK)


def decoded(code):
    code = code.astype(jnp.float32)
    for _ in range(4):
        code = lax.rsqrt(code)
    return code


def padded_2(array, sides, width):
    for axis, dim in sides:
        count, length = (lax.axis_size(axis), array.shape[dim])
        up = [(i, (i + 1) % count) for i in range(count - 1)]
        down = [(j, i) for i, j in up]
        last = lax.slice_in_dim(array, length - width, length, axis=dim)
        first = lax.slice_in_dim(array, 0, width, axis=dim)
        before = lax.ppermute(last, axis, up)
        after = lax.ppermute(first, axis, down)
        array = jnp.concatenate([before, array, after], axis=dim)
    return array


def gauss_weights(out_index, in_index, length):
    offset = out_index[:, None] - in_index[None, :]
    inside = (jnp.abs(offset) <= RADIUS) & (in_index[None, :] >= 0.0) & (in_index[None, :] < length)
    weights = jnp.where(inside, jnp.exp(-offset * offset / (2.0 * SIGMA * SIGMA)), 0.0)
    return weights / jnp.sum(weights, axis=1, keepdims=True)


def gauss_table(length):
    index = np.arange(length, dtype=np.float64)
    offset = index[:, None] - index[None, :]
    weights = np.where(np.abs(offset) <= RADIUS, np.exp(-offset * offset / (2.0 * SIGMA * SIGMA)), 0.0)
    return weights / np.sum(weights, axis=1, keepdims=True)


def halves(table):
    table = table.astype(np.float32)
    high = table.astype(jnp.bfloat16)
    low = (table - high.astype(np.float32)).astype(jnp.bfloat16)
    return np.stack([high, low])


def row_tables(height, strips):
    rows = height // strips
    gap = -rows % 16
    table = np.pad(gauss_table(height), ((0, 0), (RADIUS, RADIUS)))
    out = []
    for s in range(strips):
        own = table[s * rows:(s + 1) * rows]
        first = s * rows + RADIUS
        out.append(halves(np.concatenate([
            own[:, first:first + rows], np.zeros((rows, gap)),
            own[:, first - RADIUS:first], own[:, first + rows:first + rows + RADIUS]], axis=1)))
    return np.stack(out)


def column_tiles(width):
    padded = -(-width // LANES) * LANES
    table = np.pad(gauss_table(width).T, ((0, padded - width), (0, padded + WIDE - width)))
    tables, plan = [], []
    for w in range(0, padded, WIDE):
        start = min(max(w - LANES, 0), padded - REACH)
        block = halves(table[start:start + REACH, w:w + WIDE])
        same = [i for i, other in enumerate(tables) if np.array_equal(block, other)]
        if not same:
            tables.append(block)
        plan.append((w, min(WIDE, padded - w), min(WIDE, width - w), start, same[0] if same else len(tables) - 1))
    return np.stack(tables), plan


def split(value):
    high = value.astype(jnp.bfloat16)
    return high, (value - high.astype(jnp.float32)).astype(jnp.bfloat16)


def product(a, b):
    dot = functools.partial(jnp.dot, preferred_element_type=jnp.float32)
    return dot(a[0], b[0]) + (dot(a[0], b[1]) + dot(a[1], b[0]))


def at(strip, plate):
    return {"strip": strip, "plate": plate}


def levels_first(c):
    return c == 2


def quotient(turned, c, x_ref, out_ref):
    strips, rows, width = turned.shape[1] * 2, turned.shape[3], turned.shape[4]

    def part(w, wide):
        at_w = pl.ds(w, wide)
        below = jnp.transpose(turned[c, :, :, :, at_w].reshape(strips * rows, wide)).astype(jnp.float32)
        out_ref[at_w, :] = (x_ref[c, at_w, :].astype(jnp.float32) / below).astype(out_ref.dtype)

    full = width // LANES

    @pl.loop(0, full)
    def _(i):
        part(pl.multiple_of(i * LANES, LANES), LANES)

    if width % LANES:
        part(full * LANES, width % LANES)


def fused_kernel(plan, x_ref, gain_ref, kh_ref, kw_ref, out_ref, illum_ref, mean_ref, turned,
                 sib, ybuf, zbuf, halo, gain, kh, kw, padded, rowed,
                 load_sem, weight_sem, freed, sib_send, sib_recv, y_send, y_recv, z_send, z_recv,
                 h_send, h_recv, m_send, m_recv, i_send, i_recv, g_send, g_recv):
    channels, nz, _, rows, width = turned.shape
    strips = nz * 2
    strip, plate = lax.axis_index("strip"), lax.axis_index("plate")
    y, z = lax.rem(strip, 2), lax.div(strip, 2)
    owner = y == plate
    smoother = jnp.logical_not(owner)
    line = 1 - plate
    has_before, has_after = strip >= 1, strip + 1 < strips
    sibling, across = at(strip, 1 - plate), at(z * 2 + 1 - y, plate)
    diagonal = at(lax.rem(strip + 2 * y - 1 + strips, strips), plate)
    gap = padded.shape[1] - 2 * RADIUS
    upper, lower = at(lax.rem(strip + 2, strips), plate), at(lax.rem(strip + strips - 2, strips), plate)

    def remote(src, dst, send, recv, target):
        return pltpu.make_async_remote_copy(src, dst, send, recv, device_id=target, device_id_type=MESH)

    def load(c):
        return pltpu.make_async_copy(x_ref.at[c], out_ref.at[c], load_sem.at[c])

    def weights():
        return [pltpu.make_async_copy(gain_ref, gain, weight_sem.at[0]),
                pltpu.make_async_copy(kh_ref.at[strip], kh, weight_sem.at[1]),
                pltpu.make_async_copy(kw_ref, kw, weight_sem.at[2])]

    def to_sibling(c):
        return remote(turned.at[c, :, 1 - plate], sib.at[c], sib_send.at[c], sib_recv.at[c], sibling)

    def over(c, k):
        return remote(sib.at[c, k], ybuf.at[c, k], y_send.at[c, k], y_recv.at[c, k], across)

    def turn_of(i):
        down = nz - 1 - i
        return jnp.where(z * 2 < nz, down - (down <= z).astype(jnp.int32), i + (i >= z).astype(jnp.int32))

    def chain(c, k, up):
        slot = k + 1 if up else k
        return remote(sib.at[c, k], zbuf.at[c, slot], z_send.at[c, slot], z_recv.at[c, slot],
                      upper if up else lower)

    def halo_up(c):
        return remote(halo.at[c, 1], halo.at[c, 0], h_send.at[c, 1], h_recv.at[c, 0],
                      at(lax.rem(strip + 1, strips), plate))

    def halo_down(c):
        return remote(halo.at[c, 0], halo.at[c, 1], h_send.at[c, 0], h_recv.at[c, 1],
                      at(lax.rem(strip + strips - 1, strips), plate))

    def share_mean(c):
        return remote(mean_ref.at[c], mean_ref.at[c], m_send.at[c], m_recv.at[c], sibling)

    def share_illum(c):
        return remote(illum_ref.at[c], illum_ref.at[c], i_send.at[c], i_recv.at[c], sibling)

    def gather(c, k, kind):
        target = (sibling, across, upper, lower)[kind]
        slot = turned.at[c, k, line]
        return remote(slot, slot, g_send.at[c, k, kind], g_recv.at[c, k, line], target)

    def gathered(c, k):
        slot = turned.at[c, k, plate]
        return remote(slot, slot, g_send.at[c, k, 0], g_recv.at[c, k, plate], sibling)

    def turn(c):
        load(c).wait()
        for w in range(0, width, WIDE):
            wide = min(WIDE, width - w)
            block = jnp.transpose(out_ref[c, pl.ds(w, wide), :])
            for k in range(strips):
                turned[c, k // 2, k % 2, :, pl.ds(w, wide)] = block[k * rows:(k + 1) * rows]

    def paired(c, k, r):
        at_r = pl.ds(r, ROWS)
        return turned[c, k, plate, at_r, :].astype(jnp.float32) + sib[c, k, at_r, :].astype(jnp.float32)

    def release(c):
        to_sibling(c).wait_send()
        pl.semaphore_signal(freed.at[c], inc=1, device_id=sibling, device_id_type=MESH)

    def encode(c):
        to_sibling(c).wait_recv()
        release(c)

        def strip_sum(k):
            for r in range(0, rows, ROWS):
                sib[c, k, pl.ds(r, ROWS), :] = coded(paired(c, k, r) * 0.5)

        @pl.loop(0, nz)
        def _(i):
            k = jnp.where(i < nz - 1, turn_of(i), z)
            strip_sum(k)
            pl.when(i == 0)(lambda: pl.semaphore_wait(freed.at[c], 1))
            over(c, k).start()

    def summed(c, k, r):
        return paired(c, k, r) + 2.0 * decoded(ybuf[c, k, pl.ds(r, ROWS), :])

    def pass_on(c, count, term):
        def passed_on(k, up):
            levels = z if up else nz - 1 - z
            before = count * levels.astype(jnp.float32)
            scale = 1.0 / (before + count)

            @pl.when(levels > 0)
            def _():
                chain(c, k, up).wait_recv()
                for r in range(0, rows, ROWS):
                    at_r = pl.ds(r, ROWS)
                    value = term(c, k, r) + before * decoded(zbuf[c, k + 1 if up else k, at_r, :])
                    sib[c, k, at_r, :] = coded(value * scale)

            @pl.when(levels == 0)
            def _():
                for r in range(0, rows, ROWS):
                    sib[c, k, pl.ds(r, ROWS), :] = coded(term(c, k, r) * scale)

            chain(c, k, up).start()

        @pl.loop(0, nz - 1)
        def _(i):
            k = turn_of(i)
            if term is summed:
                over(c, k).wait_recv()
            pl.when(k > z)(lambda: passed_on(k, True))
            pl.when(k < z)(lambda: passed_on(k, False))

    def add_levels(c, count, sum_ref):
        def add(up):
            chain(c, z, up).wait_recv()
            weight = count * (z if up else nz - 1 - z).astype(jnp.float32)
            for r in range(0, rows, ROWS):
                at_r = pl.ds(r, ROWS)
                sum_ref[c, at_r, :] += weight * decoded(zbuf[c, z + 1 if up else z, at_r, :])

        pl.when(z >= 1)(lambda: add(True))
        pl.when(z + 1 < nz)(lambda: add(False))

    def column_sums(c, sum_ref):
        to_sibling(c).wait_recv()
        pl.when(smoother)(lambda: release(c))
        pl.semaphore_wait(freed.at[c], 1)
        pass_on(c, 2.0, paired)
        for r in range(0, rows, ROWS):
            sum_ref[c, pl.ds(r, ROWS), :] = paired(c, z, r)

    def encode_column(c):
        column_sums(c, illum_ref)
        add_levels(c, 2.0, illum_ref)
        for r in range(0, rows, ROWS):
            at_r = pl.ds(r, ROWS)
            sib[c, z, at_r, :] = coded(illum_ref[c, at_r, :] * (1.0 / strips))
        over(c, z).start()

    def across_sums(c):
        to_sibling(c).wait_recv()
        pl.semaphore_wait(freed.at[c], 1)
        pass_on(c, 4.0, summed)
        over(c, z).wait_recv()
        for r in range(0, rows, ROWS):
            mean_ref[c, pl.ds(r, ROWS), :] = summed(c, z, r)

    def finish_mean(c):
        pl.when(jnp.logical_not(levels_first(c)))(lambda: add_levels(c, 4.0, mean_ref))

        @pl.when(levels_first(c))
        def _():
            add_levels(c, 2.0, mean_ref)
            over(c, z).wait_recv()
            for r in range(0, rows, ROWS):
                at_r = pl.ds(r, ROWS)
                mean_ref[c, at_r, :] += strips * decoded(ybuf[c, z, at_r, :])

        for r in range(0, rows, ROWS):
            at_r = pl.ds(r, ROWS)
            value = mean_ref[c, at_r, :]
            value = value * (1.0 / (2 * strips))
            mean_ref[c, at_r, :] = value
            if r < RADIUS:
                halo[c, 0, at_r, :] = coded(value)
            if r >= rows - RADIUS:
                halo[c, 1, pl.ds(r - rows + RADIUS, ROWS), :] = coded(value)
        pl.when(has_after)(lambda: halo_up(c).start())
        pl.when(has_before)(lambda: halo_down(c).start())
        share_mean(c).start()

    def fill(r, value):
        at_r = pl.ds(r, value.shape[0])
        high, low = split(value)
        padded[0, at_r, pl.ds(0, width)] = high
        padded[1, at_r, pl.ds(0, width)] = low

    def smooth(c):
        share_mean(c).wait_recv()
        for r in range(0, rows, ROWS):
            fill(r, mean_ref[c, pl.ds(r, ROWS), :])

        @pl.when(has_before)
        def _():
            halo_up(c).wait_recv()
            for r in range(0, RADIUS, ROWS):
                fill(gap + r, decoded(halo[c, 0, pl.ds(r, ROWS), :]))

        @pl.when(has_after)
        def _():
            halo_down(c).wait_recv()
            for r in range(0, RADIUS, ROWS):
                fill(gap + RADIUS + r, decoded(halo[c, 1, pl.ds(r, ROWS), :]))

        for w, wide, _, _, _ in plan:
            cols = pl.ds(w, wide)
            value = product((kh[0], kh[1]), (padded[0, :, cols], padded[1, :, cols]))
            rowed[0, :, cols], rowed[1, :, cols] = split(value)

        for w, wide, used, start, index in plan:
            reach = pl.ds(start, REACH)
            value = product((rowed[0, :, reach], rowed[1, :, reach]),
                            (kw[index, 0, :, pl.ds(0, wide)], kw[index, 1, :, pl.ds(0, wide)]))[:, :used]
            cols = pl.ds(w, used)
            illum_ref[c, :, cols] = value
            turned[c, z, y, :, cols] = (value * gain[c, :, cols].astype(jnp.float32)).astype(jnp.bfloat16)
        pl.when(z + 1 < nz)(lambda: gather(c, z, 2).start())
        pl.when(z >= 1)(lambda: gather(c, z, 3).start())
        gather(c, z, 1).start()
        gather(c, z, 0).start()
        share_illum(c).start()

    def relay(c):
        @pl.loop(0, nz)
        def _(d):
            @pl.when((z - d >= 0) & ((d > 0) | owner))
            def _():
                k = z - d
                gather(c, k, 0).wait_recv()
                pl.when(smoother & (z + 1 < nz))(lambda: gather(c, k, 2).start())
                pl.when(smoother)(lambda: gather(c, k, 1).start())
                gather(c, k, 0).start()

            @pl.when((z + d < nz) & (d > 0))
            def _():
                k = z + d
                gather(c, k, 0).wait_recv()
                pl.when(smoother & (z >= 1))(lambda: gather(c, k, 3).start())
                pl.when(smoother)(lambda: gather(c, k, 1).start())
                gather(c, k, 0).start()

    def divide(c):
        @pl.loop(0, nz)
        def _(k):
            gathered(c, k).wait_recv()

        pl.when(c + 1 < channels)(lambda: quotient(turned, c, out_ref, out_ref.at[c]))

    partners = [sibling, across, diagonal] + [upper, lower]
    load(0).start()
    barrier = pltpu.get_barrier_semaphore()
    for partner in partners:
        pl.semaphore_signal(barrier, inc=1, device_id=partner, device_id_type=MESH)
    load(1).start()
    turn(0)
    pl.semaphore_wait(barrier, len(partners))
    to_sibling(0).start()
    for c in range(2, channels):
        load(c).start()
    for copy in weights():
        copy.start()

    def order(t):
        return t + (t == 2).astype(jnp.int32) - (t == 3).astype(jnp.int32)

    def turn_and_send(c):
        turn(c)
        to_sibling(c).start()

    @pl.when(smoother)
    def _():
        padded[...] = jnp.zeros_like(padded)

        @pl.loop(0, channels)
        def _(t):
            pl.when(t + 1 < channels)(lambda: turn_and_send(t + 1))
            c = order(t)
            pl.when(levels_first(c))(lambda: encode_column(c))
            pl.when(jnp.logical_not(levels_first(c)))(lambda: encode(c))

        for copy in weights():
            copy.wait()

        @pl.loop(0, channels + 2)
        def _(c):
            pl.when(c < channels)(lambda: smooth(c))
            pl.when((c >= 1) & (c <= channels))(lambda: relay(c - 1))
            pl.when(c >= 2)(lambda: divide(c - 2))

    @pl.when(owner)
    def _():
        @pl.loop(1, channels + 1)
        def _(c):
            pl.when(c < channels)(lambda: turn_and_send(c))
            release(c - 1)

        @pl.loop(0, channels * 2)
        def _(c):
            pl.when((c < channels) & jnp.logical_not(levels_first(c)))(lambda: across_sums(c))
            pl.when((c < channels) & levels_first(c))(lambda: column_sums(c, mean_ref))
            pl.when((c >= 1) & (c <= channels))(lambda: finish_mean(c - 1))
            pl.when((c >= 4) & (c < channels + 4))(lambda: relay(c - 4))
            pl.when(c >= 5)(lambda: divide(c - 5))

        for copy in weights():
            copy.wait()

        @pl.loop(0, channels)
        def _(c):
            share_illum(c).wait_recv()

    @pl.loop(0, channels)
    def _(c):
        @pl.when(smoother)
        def _():
            share_illum(c).wait_send()

            @pl.loop(0, nz)
            def _(k):
                pl.when((k == z) | jnp.logical_not(levels_first(c)))(lambda: over(c, k).wait_send())

        @pl.when(owner)
        def _():
            share_mean(c).wait_send()
            pl.when(has_after)(lambda: halo_up(c).wait_send())
            pl.when(has_before)(lambda: halo_down(c).wait_send())

        chained = owner | levels_first(c)

        @pl.loop(0, nz)
        def _(k):
            pl.when(chained & (k > z))(lambda: chain(c, k, True).wait_send())
            pl.when(chained & (k < z))(lambda: chain(c, k, False).wait_send())
            gather(c, k, 0).wait_send()
            pl.when(smoother)(lambda: gather(c, k, 1).wait_send())
            pl.when(smoother & (k <= z) & (z + 1 < nz))(lambda: gather(c, k, 2).wait_send())
            pl.when(smoother & (k >= z) & (z >= 1))(lambda: gather(c, k, 3).wait_send())


def fused(x, gain, strips):
    channels, width, height = x.shape
    rows, nz = height // strips, strips // 2
    padded_width = -(-width // LANES) * LANES
    kh = row_tables(height, strips)
    kw, plan = column_tiles(width)
    dma = pltpu.SemaphoreType.DMA
    each, levels, chains = dma((channels,)), dma((channels, nz)), dma((channels, nz + 1))
    part = (channels, nz, rows, width)
    own = (channels, rows, width)
    anywhere = pl.BlockSpec(memory_space=pl.ANY)
    held = [pltpu.VMEM(x.shape, x.dtype), pltpu.VMEM(own, jnp.float32), pltpu.VMEM(own, jnp.float32),
            pltpu.VMEM((channels, nz, 2, rows, width), x.dtype)]
    return pl.pallas_call(
        functools.partial(fused_kernel, plan),
        out_shape=held,
        in_specs=[anywhere] * 4,
        out_specs=[pl.BlockSpec(memory_space=pltpu.VMEM)] * 4,
        scratch_shapes=[
            pltpu.VMEM(part, LINK),
            pltpu.VMEM(part, LINK),
            pltpu.VMEM((channels, nz + 1, rows, width), LINK),
            pltpu.VMEM((channels, 2, RADIUS, width), LINK),
            pltpu.VMEM(own, gain.dtype),
            pltpu.VMEM(kh.shape[1:], jnp.bfloat16),
            pltpu.VMEM(kw.shape, jnp.bfloat16),
            pltpu.VMEM((2, kh.shape[3], padded_width), jnp.bfloat16),
            pltpu.VMEM((2, rows, padded_width), jnp.bfloat16),
            each, dma((3,)), pltpu.SemaphoreType.REGULAR((channels,)), each, each, levels, levels, chains, chains,
            dma((channels, 2)), dma((channels, 2)), each, each, each, each,
            dma((channels, nz, 4)), dma((channels, nz, 2)),
        ],
        compiler_params=pltpu.CompilerParams(
            collective_id=0, has_side_effects=True, vmem_limit_bytes=34 * 2**20),
        name="fused",
    )(x, gain, kh, kw)


def stored_kernel(divided, illum, mean, turned, *refs):
    targets, last, sems = refs[:3], refs[3], refs[4]
    channels = divided.shape[0]
    copies = [pltpu.make_async_copy(source.at[c], target.at[c], sems.at[i, c])
              for i, (source, target) in enumerate(zip((divided, illum, mean), targets))
              for c in range(channels) if i or c + 1 < channels]
    for copy in copies:
        copy.start()
    quotient(turned, channels - 1, divided, last)
    copies.append(pltpu.make_async_copy(last, targets[0].at[channels - 1], sems.at[0, channels - 1]))
    copies[-1].start()
    for copy in copies:
        copy.wait()


def stored(arrays):
    anywhere = pl.BlockSpec(memory_space=pl.ANY)
    channels, width, height = arrays[0].shape
    return pl.pallas_call(
        stored_kernel,
        out_shape=[jax.ShapeDtypeStruct(a.shape, a.dtype) for a in arrays[:3]],
        in_specs=[pl.BlockSpec(memory_space=pltpu.VMEM)] * 4,
        out_specs=[anywhere] * 3,
        scratch_shapes=[pltpu.VMEM((width, height), arrays[0].dtype), pltpu.SemaphoreType.DMA((3, channels))],
        compiler_params=pltpu.CompilerParams(vmem_limit_bytes=16 * 2**20),
        name="stored",
    )(*arrays)


def on_grid(fields, flat_gain):
    x = jnp.transpose(fields[0], (1, 2, 0))
    gain = jnp.transpose(flat_gain, (1, 0, 2))
    corrected, illumination, mean_field = stored(fused(x, gain, lax.axis_size("strip")))
    back = lambda a: jnp.transpose(a, (1, 0, 2))
    return (jnp.transpose(corrected, (2, 0, 1))[None], back(illumination), back(mean_field))


def on_device(fields, flat_gain):
    num_fields, height, channels, width = fields.shape
    strips = lax.axis_size("strip")
    plates = lax.axis_size("plate")
    strip_rows = height // strips
    count = num_fields * strips * plates
    block = fields
    partial_sum = lax.psum_scatter(
        jnp.sum(block, axis=0, dtype=jnp.float32), "strip", scatter_dimension=0, tiled=True
    )
    total = lax.psum(partial_sum, "plate")
    mean_field = total / count
    col_index = jnp.arange(width, dtype=jnp.float32)
    col_kernel = gauss_weights(col_index, col_index, float(width))
    smooth_cols = jnp.einsum("hcv,wv->hcw", mean_field, col_kernel, precision=lax.Precision.HIGHEST)
    padded = padded_2(smooth_cols, (("strip", 0),), RADIUS)
    first_row = (lax.axis_index("strip") * strip_rows).astype(jnp.float32)
    out_index = first_row + jnp.arange(strip_rows, dtype=jnp.float32)
    in_index = first_row - RADIUS + jnp.arange(strip_rows + 2 * RADIUS, dtype=jnp.float32)
    row_kernel = gauss_weights(out_index, in_index, float(height))
    illumination = jnp.einsum("hu,ucw->hcw", row_kernel, padded, precision=lax.Precision.HIGHEST)
    illum_round = (illumination * flat_gain.astype(jnp.float32)).astype(jnp.bfloat16)
    block = fields
    corrected = (
        block.astype(jnp.float32)
        / lax.all_gather(illum_round, "strip", axis=0, tiled=True).astype(jnp.float32)[None]
    ).astype(jnp.bfloat16)
    return (corrected, illumination, mean_field)


def solution(mesh):
    grid = mesh.shape["strip"] == 8 and mesh.shape["plate"] == 2
    return jax.shard_map(
        on_grid if grid else on_device,
        mesh=mesh,
        in_specs=(P(("batch", "strip", "plate"), None, None, None), P("strip", None, None)),
        out_specs=(
            P(("batch", "strip", "plate"), None, None, None),
            P("strip", "batch", None),
            P("strip", "batch", None),
        ),
        check_vma=False,
    )
```

```python
import functools
import jax
import jax.numpy as jnp
import numpy as np
from jax import lax
from jax.experimental import pallas as pl
from jax.experimental.pallas import tpu as pltpu
from jax.sharding import PartitionSpec as P

SIGMA = 16
RADIUS = 48
ROWS = 8
WIDE = 256
REACH = 512
LANES = 128
CHUNK = 40
MESH = pl.DeviceIdType.MESH
LINK = jnp.bfloat16


def coded(mean):
    for _ in range(4):
        mean = mean * mean
    return mean.astype(LINK)


def decoded(code):
    code = code.astype(jnp.float32)
    for _ in range(4):
        code = lax.rsqrt(code)
    return code


def padded_2(array, sides, width):
    for axis, dim in sides:
        count, length = (lax.axis_size(axis), array.shape[dim])
        up = [(i, (i + 1) % count) for i in range(count - 1)]
        down = [(j, i) for i, j in up]
        last = lax.slice_in_dim(array, length - width, length, axis=dim)
        first = lax.slice_in_dim(array, 0, width, axis=dim)
        before = lax.ppermute(last, axis, up)
        after = lax.ppermute(first, axis, down)
        array = jnp.concatenate([before, array, after], axis=dim)
    return array


def gauss_weights(out_index, in_index, length):
    offset = out_index[:, None] - in_index[None, :]
    inside = (jnp.abs(offset) <= RADIUS) & (in_index[None, :] >= 0.0) & (in_index[None, :] < length)
    weights = jnp.where(inside, jnp.exp(-offset * offset / (2.0 * SIGMA * SIGMA)), 0.0)
    return weights / jnp.sum(weights, axis=1, keepdims=True)


def gauss_table(length):
    index = np.arange(length, dtype=np.float64)
    offset = index[:, None] - index[None, :]
    weights = np.where(np.abs(offset) <= RADIUS, np.exp(-offset * offset / (2.0 * SIGMA * SIGMA)), 0.0)
    return weights / np.sum(weights, axis=1, keepdims=True)


def halves(table):
    table = table.astype(np.float32)
    high = table.astype(jnp.bfloat16)
    low = (table - high.astype(np.float32)).astype(jnp.bfloat16)
    return np.stack([high, low])


def row_tables(height, strips):
    rows = height // strips
    gap = -rows % 16
    table = np.pad(gauss_table(height), ((0, 0), (RADIUS, RADIUS)))
    out = []
    for s in range(strips):
        own = table[s * rows:(s + 1) * rows]
        first = s * rows + RADIUS
        out.append(halves(np.concatenate([
            own[:, first:first + rows], np.zeros((rows, gap)),
            own[:, first - RADIUS:first], own[:, first + rows:first + rows + RADIUS]], axis=1)))
    return np.stack(out)


def column_tiles(width):
    padded = -(-width // LANES) * LANES
    table = np.pad(gauss_table(width).T, ((0, padded - width), (0, padded + WIDE - width)))
    tables, plan = [], []
    for w in range(0, padded, WIDE):
        start = min(max(w - LANES, 0), padded - REACH)
        block = halves(table[start:start + REACH, w:w + WIDE])
        same = [i for i, other in enumerate(tables) if np.array_equal(block, other)]
        if not same:
            tables.append(block)
        plan.append((w, min(WIDE, padded - w), min(WIDE, width - w), start, same[0] if same else len(tables) - 1))
    return np.stack(tables), plan


def split(value):
    high = value.astype(jnp.bfloat16)
    return high, (value - high.astype(jnp.float32)).astype(jnp.bfloat16)


def product(a, b):
    dot = functools.partial(jnp.dot, preferred_element_type=jnp.float32)
    return dot(a[0], b[0]) + (dot(a[0], b[1]) + dot(a[1], b[0]))


def at(strip, plate):
    return {"strip": strip, "plate": plate}


def levels_first(c):
    return c == 2


def packing(rows, width):
    full, rest = divmod(width, LANES)
    fold = -(-rows // 16) * 8
    return full, rest, fold, full * rows + fold


def unpack(rows, width, get, put):
    full, rest, fold, _ = packing(rows, width)
    for j in range(full):
        put(pl.ds(0, rows), pl.ds(j * LANES, LANES), get(pl.ds(j * rows, rows)))
    tail = get(pl.ds(full * rows, fold))
    at_rest = pl.ds(full * LANES, rest)
    put(pl.ds(0, fold), at_rest, tail[:, :rest])
    put(pl.ds(fold, rows - fold), at_rest, pltpu.roll(tail, LANES // 2, 1)[:rows - fold, :rest])


def quotient(turned, c, rows, x_ref, out_ref):
    strips, width = turned.shape[1] * 2, x_ref.shape[1]
    full, rest, fold, _ = packing(rows, width)

    def part(at_w, below):
        out_ref[at_w, :] = (x_ref[c, at_w, :].astype(jnp.float32) / below).astype(out_ref.dtype)

    for j in range(full):
        block = turned[c, :, :, pl.ds(j * rows, rows), :].reshape(strips * rows, LANES)
        part(pl.ds(j * LANES, LANES), jnp.transpose(block).astype(jnp.float32))
    pieces = []
    for k in range(strips):
        tail = turned[c, k // 2, k % 2, pl.ds(full * rows, fold), :].astype(jnp.float32)
        pieces += [tail, pltpu.roll(tail, LANES // 2, 1)[:rows - fold]]
    part(pl.ds(full * LANES, rest), jnp.transpose(jnp.concatenate(pieces, axis=0))[:rest])


def fused_kernel(plan, x_ref, gain_ref, kh_ref, kw_ref, out_ref, illum_ref, mean_ref, turned,
                 sib, ybuf, zbuf, halo, gain, kh, kw, padded, rowed, partial, edge,
                 load_sem, weight_sem, freed, sib_send, sib_recv, y_send, y_recv, z_send, z_recv,
                 h_send, h_recv, m_send, m_recv, i_send, i_recv, g_send, g_recv):
    channels, rows, width = mean_ref.shape
    nz = turned.shape[1]
    full, rest, fold, depth = packing(rows, width)
    chunks = [pl.ds(r, min(CHUNK, depth - r)) for r in range(0, depth, CHUNK)]
    strips = nz * 2
    strip, plate = lax.axis_index("strip"), lax.axis_index("plate")
    y, z = lax.rem(strip, 2), lax.div(strip, 2)
    owner = y == plate
    smoother = jnp.logical_not(owner)
    line = 1 - plate
    has_before, has_after = strip >= 1, strip + 1 < strips
    sibling, across = at(strip, 1 - plate), at(z * 2 + 1 - y, plate)
    diagonal = at(lax.rem(strip + 2 * y - 1 + strips, strips), plate)
    gap = padded.shape[1] - 2 * RADIUS
    upper, lower = at(lax.rem(strip + 2, strips), plate), at(lax.rem(strip + strips - 2, strips), plate)

    def remote(src, dst, send, recv, target):
        return pltpu.make_async_remote_copy(src, dst, send, recv, device_id=target, device_id_type=MESH)

    def load(c):
        return pltpu.make_async_copy(x_ref.at[c], out_ref.at[c], load_sem.at[c])

    def weights():
        return [pltpu.make_async_copy(gain_ref, gain, weight_sem.at[0]),
                pltpu.make_async_copy(kh_ref.at[strip], kh, weight_sem.at[1]),
                pltpu.make_async_copy(kw_ref, kw, weight_sem.at[2])]

    def to_sibling(c):
        return remote(turned.at[c, :, 1 - plate], sib.at[c], sib_send.at[c], sib_recv.at[c], sibling)

    def over(c, k):
        return remote(sib.at[c, k], ybuf.at[c, k], y_send.at[c, k], y_recv.at[c, k], across)

    def turn_of(i):
        down = nz - 1 - i
        return jnp.where(z * 2 < nz, down - (down <= z).astype(jnp.int32), i + (i >= z).astype(jnp.int32))

    def chain(c, k, up):
        slot = k + 1 if up else k
        return remote(sib.at[c, k], zbuf.at[c, slot], z_send.at[c, slot], z_recv.at[c, slot],
                      upper if up else lower)

    def halo_up(c):
        return remote(halo.at[c, 1], halo.at[c, 0], h_send.at[c, 1], h_recv.at[c, 0],
                      at(lax.rem(strip + 1, strips), plate))

    def halo_down(c):
        return remote(halo.at[c, 0], halo.at[c, 1], h_send.at[c, 0], h_recv.at[c, 1],
                      at(lax.rem(strip + strips - 1, strips), plate))

    def share_mean(c):
        return remote(mean_ref.at[c], mean_ref.at[c], m_send.at[c], m_recv.at[c], sibling)

    def share_illum(c):
        return remote(illum_ref.at[c], illum_ref.at[c], i_send.at[c], i_recv.at[c], sibling)

    def gather(c, k, kind):
        target = (sibling, across, upper, lower)[kind]
        slot = turned.at[c, k, line]
        return remote(slot, slot, g_send.at[c, k, kind], g_recv.at[c, k, line], target)

    def gathered(c, k):
        slot = turned.at[c, k, plate]
        return remote(slot, slot, g_send.at[c, k, 0], g_recv.at[c, k, plate], sibling)

    def turn(c):
        load(c).wait()
        for j in range(full):
            block = jnp.transpose(out_ref[c, pl.ds(j * LANES, LANES), :])
            for k in range(strips):
                turned[c, k // 2, k % 2, pl.ds(j * rows, rows), :] = block[k * rows:(k + 1) * rows]
        near = full * LANES - LANES // 2
        both = jnp.transpose(out_ref[c, pl.ds(near, width - near), :])
        ends = jnp.transpose(out_ref[c, pl.ds(full * LANES, rest), :])
        for k in range(strips):
            slot = turned.at[c, k // 2, k % 2]
            slot[pl.ds(full * rows, rows - fold), pl.ds(0, width - near)] = both[k * rows + fold:(k + 1) * rows]
            slot[pl.ds(full * rows, fold), pl.ds(0, rest)] = ends[k * rows:k * rows + fold]

    def paired(c, k, at_r):
        return turned[c, k, plate, at_r, :].astype(jnp.float32) + sib[c, k, at_r, :].astype(jnp.float32)

    def release(c):
        to_sibling(c).wait_send()
        pl.semaphore_signal(freed.at[c], inc=1, device_id=sibling, device_id_type=MESH)

    def encode(c):
        to_sibling(c).wait_recv()
        release(c)

        def strip_sum(k):
            for at_r in chunks:
                sib[c, k, at_r, :] = coded(paired(c, k, at_r) * 0.5)

        @pl.loop(0, nz)
        def _(i):
            k = jnp.where(i < nz - 1, turn_of(i), z)
            strip_sum(k)
            pl.when(i == 0)(lambda: pl.semaphore_wait(freed.at[c], 1))
            over(c, k).start()

    def summed(c, k, at_r):
        return paired(c, k, at_r) + 2.0 * decoded(ybuf[c, k, at_r, :])

    def pass_on(c, count, term):
        def passed_on(k, up):
            levels = z if up else nz - 1 - z
            before = count * levels.astype(jnp.float32)
            scale = 1.0 / (before + count)

            @pl.when(levels > 0)
            def _():
                chain(c, k, up).wait_recv()
                for at_r in chunks:
                    value = term(c, k, at_r) + before * decoded(zbuf[c, k + 1 if up else k, at_r, :])
                    sib[c, k, at_r, :] = coded(value * scale)

            @pl.when(levels == 0)
            def _():
                for at_r in chunks:
                    sib[c, k, at_r, :] = coded(term(c, k, at_r) * scale)

            chain(c, k, up).start()

        @pl.loop(0, nz - 1)
        def _(i):
            k = turn_of(i)
            if term is summed:
                over(c, k).wait_recv()
            pl.when(k > z)(lambda: passed_on(k, True))
            pl.when(k < z)(lambda: passed_on(k, False))

    def into_mean(c, get):
        def put(at_r, cols, value):
            mean_ref[c, at_r, cols] = value

        unpack(rows, width, get, put)

    def onto_mean(c, get):
        def put(at_r, cols, value):
            mean_ref[c, at_r, cols] += value

        unpack(rows, width, get, put)

    def onto_partial(c, get):
        for at_r in chunks:
            partial[at_r, :] += get(at_r)

    def add_levels(c, count, onto):
        def add(up):
            chain(c, z, up).wait_recv()
            weight = count * (z if up else nz - 1 - z).astype(jnp.float32)
            onto(c, lambda at_r: weight * decoded(zbuf[c, z + 1 if up else z, at_r, :]))

        pl.when(z >= 1)(lambda: add(True))
        pl.when(z + 1 < nz)(lambda: add(False))

    def pass_column(c):
        to_sibling(c).wait_recv()
        pl.when(smoother)(lambda: release(c))
        pl.semaphore_wait(freed.at[c], 1)
        pass_on(c, 2.0, paired)

    def column_sums(c):
        pass_column(c)
        into_mean(c, lambda at_r: paired(c, z, at_r))

    def encode_column(c):
        pass_column(c)
        for at_r in chunks:
            partial[at_r, :] = paired(c, z, at_r)
        add_levels(c, 2.0, onto_partial)
        for at_r in chunks:
            sib[c, z, at_r, :] = coded(partial[at_r, :] * (1.0 / strips))
        over(c, z).start()

    def across_sums(c):
        to_sibling(c).wait_recv()
        pl.semaphore_wait(freed.at[c], 1)
        pass_on(c, 4.0, summed)
        over(c, z).wait_recv()
        into_mean(c, lambda at_r: summed(c, z, at_r))

    def finish_mean(c):
        pl.when(jnp.logical_not(levels_first(c)))(lambda: add_levels(c, 4.0, onto_mean))

        @pl.when(levels_first(c))
        def _():
            add_levels(c, 2.0, onto_mean)
            over(c, z).wait_recv()
            onto_mean(c, lambda at_r: strips * decoded(ybuf[c, z, at_r, :]))

        for r in range(0, rows, ROWS):
            at_r = pl.ds(r, ROWS)
            value = mean_ref[c, at_r, :]
            value = value * (1.0 / (2 * strips))
            mean_ref[c, at_r, :] = value
            if r < RADIUS:
                halo[c, 0, at_r, :] = coded(value)
            if r >= rows - RADIUS:
                halo[c, 1, pl.ds(r - rows + RADIUS, ROWS), :] = coded(value)
        pl.when(has_after)(lambda: halo_up(c).start())
        pl.when(has_before)(lambda: halo_down(c).start())
        share_mean(c).start()

    def fill(r, value):
        at_r = pl.ds(r, value.shape[0])
        high, low = split(value)
        padded[0, at_r, pl.ds(0, width)] = high
        padded[1, at_r, pl.ds(0, width)] = low

    def smooth(c):
        share_mean(c).wait_recv()
        for r in range(0, rows, ROWS):
            fill(r, mean_ref[c, pl.ds(r, ROWS), :])

        @pl.when(has_before)
        def _():
            halo_up(c).wait_recv()
            for r in range(0, RADIUS, ROWS):
                fill(gap + r, decoded(halo[c, 0, pl.ds(r, ROWS), :]))

        @pl.when(has_after)
        def _():
            halo_down(c).wait_recv()
            for r in range(0, RADIUS, ROWS):
                fill(gap + RADIUS + r, decoded(halo[c, 1, pl.ds(r, ROWS), :]))

        for w, wide, _, _, _ in plan:
            cols = pl.ds(w, wide)
            value = product((kh[0], kh[1]), (padded[0, :, cols], padded[1, :, cols]))
            rowed[0, :, cols], rowed[1, :, cols] = split(value)

        for w, wide, used, start, index in plan:
            reach = pl.ds(start, REACH)
            value = product((rowed[0, :, reach], rowed[1, :, reach]),
                            (kw[index, 0, :, pl.ds(0, wide)], kw[index, 1, :, pl.ds(0, wide)]))[:, :used]
            cols = pl.ds(w, used)
            illum_ref[c, :, cols] = value
            weighted = value * gain[c, :, cols].astype(jnp.float32)
            for j in range(w // LANES, (w + used) // LANES):
                tile = weighted[:, j * LANES - w:(j + 1) * LANES - w]
                turned[c, z, y, pl.ds(j * rows, rows), :] = tile.astype(jnp.bfloat16)
            if used % LANES:
                edge[:, pl.ds(0, rest)] = weighted[:, used - rest:]
                moved = pltpu.roll(edge[pl.ds(fold, rows - fold), :], LANES // 2, 1)
                slot = turned.at[c, z, y]
                slot[pl.ds(full * rows, rows - fold), :] = moved.astype(jnp.bfloat16)
                slot[pl.ds(full * rows, fold), pl.ds(0, rest)] = edge[pl.ds(0, fold), pl.ds(0, rest)].astype(jnp.bfloat16)
        pl.when(z + 1 < nz)(lambda: gather(c, z, 2).start())
        pl.when(z >= 1)(lambda: gather(c, z, 3).start())
        gather(c, z, 1).start()
        gather(c, z, 0).start()
        share_illum(c).start()

    def relay(c):
        @pl.loop(0, nz)
        def _(d):
            @pl.when((z - d >= 0) & ((d > 0) | owner))
            def _():
                k = z - d
                gather(c, k, 0).wait_recv()
                pl.when(smoother & (z + 1 < nz))(lambda: gather(c, k, 2).start())
                pl.when(smoother)(lambda: gather(c, k, 1).start())
                gather(c, k, 0).start()

            @pl.when((z + d < nz) & (d > 0))
            def _():
                k = z + d
                gather(c, k, 0).wait_recv()
                pl.when(smoother & (z >= 1))(lambda: gather(c, k, 3).start())
                pl.when(smoother)(lambda: gather(c, k, 1).start())
                gather(c, k, 0).start()

    def divide(c):
        @pl.loop(0, nz)
        def _(k):
            gathered(c, k).wait_recv()

        quotient(turned, c, rows, out_ref, out_ref.at[c])

    partners = [sibling, across, diagonal] + [upper, lower]
    load(0).start()
    barrier = pltpu.get_barrier_semaphore()
    for partner in partners:
        pl.semaphore_signal(barrier, inc=1, device_id=partner, device_id_type=MESH)
    load(1).start()
    turn(0)
    pl.semaphore_wait(barrier, len(partners))
    to_sibling(0).start()
    for c in range(2, channels):
        load(c).start()
    for copy in weights():
        copy.start()

    def order(t):
        return t + (t == 2).astype(jnp.int32) - (t == 3).astype(jnp.int32)

    def turn_and_send(c):
        turn(c)
        to_sibling(c).start()

    @pl.when(smoother)
    def _():
        padded[...] = jnp.zeros_like(padded)

        @pl.loop(0, channels)
        def _(t):
            pl.when(t + 1 < channels)(lambda: turn_and_send(t + 1))
            c = order(t)
            pl.when(levels_first(c))(lambda: encode_column(c))
            pl.when(jnp.logical_not(levels_first(c)))(lambda: encode(c))

        for copy in weights():
            copy.wait()

        @pl.loop(0, channels + 2)
        def _(c):
            pl.when(c < channels)(lambda: smooth(c))
            pl.when((c >= 1) & (c <= channels))(lambda: relay(c - 1))
            pl.when(c >= 2)(lambda: divide(c - 2))

    @pl.when(owner)
    def _():
        @pl.loop(1, channels + 1)
        def _(c):
            pl.when(c < channels)(lambda: turn_and_send(c))
            release(c - 1)

        @pl.loop(0, channels * 2)
        def _(c):
            pl.when((c < channels) & jnp.logical_not(levels_first(c)))(lambda: across_sums(c))
            pl.when((c < channels) & levels_first(c))(lambda: column_sums(c))
            pl.when((c >= 1) & (c <= channels))(lambda: finish_mean(c - 1))
            pl.when((c >= 4) & (c < channels + 4))(lambda: relay(c - 4))
            pl.when(c >= 5)(lambda: divide(c - 5))

        for copy in weights():
            copy.wait()

        @pl.loop(0, channels)
        def _(c):
            share_illum(c).wait_recv()

    @pl.loop(0, channels)
    def _(c):
        @pl.when(smoother)
        def _():
            share_illum(c).wait_send()

            @pl.loop(0, nz)
            def _(k):
                pl.when((k == z) | jnp.logical_not(levels_first(c)))(lambda: over(c, k).wait_send())

        @pl.when(owner)
        def _():
            share_mean(c).wait_send()
            pl.when(has_after)(lambda: halo_up(c).wait_send())
            pl.when(has_before)(lambda: halo_down(c).wait_send())

        chained = owner | levels_first(c)

        @pl.loop(0, nz)
        def _(k):
            pl.when(chained & (k > z))(lambda: chain(c, k, True).wait_send())
            pl.when(chained & (k < z))(lambda: chain(c, k, False).wait_send())
            gather(c, k, 0).wait_send()
            pl.when(smoother)(lambda: gather(c, k, 1).wait_send())
            pl.when(smoother & (k <= z) & (z + 1 < nz))(lambda: gather(c, k, 2).wait_send())
            pl.when(smoother & (k >= z) & (z >= 1))(lambda: gather(c, k, 3).wait_send())


def fused(x, gain, strips):
    channels, width, height = x.shape
    rows, nz = height // strips, strips // 2
    padded_width = -(-width // LANES) * LANES
    kh = row_tables(height, strips)
    kw, plan = column_tiles(width)
    dma = pltpu.SemaphoreType.DMA
    each, levels, chains = dma((channels,)), dma((channels, nz)), dma((channels, nz + 1))
    depth = packing(rows, width)[3]
    part = (channels, nz, depth, LANES)
    own = (channels, rows, width)
    anywhere = pl.BlockSpec(memory_space=pl.ANY)
    held = [pltpu.VMEM(x.shape, x.dtype), pltpu.VMEM(own, jnp.float32), pltpu.VMEM(own, jnp.float32)]
    return pl.pallas_call(
        functools.partial(fused_kernel, plan),
        out_shape=held,
        in_specs=[anywhere] * 4,
        out_specs=[pl.BlockSpec(memory_space=pltpu.VMEM)] * 3,
        scratch_shapes=[
            pltpu.VMEM((channels, nz, 2, depth, LANES), x.dtype),
            pltpu.VMEM(part, LINK),
            pltpu.VMEM(part, LINK),
            pltpu.VMEM((channels, nz + 1, depth, LANES), LINK),
            pltpu.VMEM((channels, 2, RADIUS, width), LINK),
            pltpu.VMEM(own, gain.dtype),
            pltpu.VMEM(kh.shape[1:], jnp.bfloat16),
            pltpu.VMEM(kw.shape, jnp.bfloat16),
            pltpu.VMEM((2, kh.shape[3], padded_width), jnp.bfloat16),
            pltpu.VMEM((2, rows, padded_width), jnp.bfloat16),
            pltpu.VMEM((depth, LANES), jnp.float32),
            pltpu.VMEM((rows, LANES), jnp.float32),
            each, dma((3,)), pltpu.SemaphoreType.REGULAR((channels,)), each, each, levels, levels, chains, chains,
            dma((channels, 2)), dma((channels, 2)), each, each, each, each,
            dma((channels, nz, 4)), dma((channels, nz, 2)),
        ],
        compiler_params=pltpu.CompilerParams(
            collective_id=0, has_side_effects=True, vmem_limit_bytes=45 * 2**20),
        name="fused",
    )(x, gain, kh, kw)


def stored_kernel(*refs):
    sources, targets, sems = refs[:3], refs[3:6], refs[6]
    copies = [pltpu.make_async_copy(source.at[c], target.at[c], sems.at[i, c])
              for i, (source, target) in enumerate(zip(sources, targets)) for c in range(source.shape[0])]
    for copy in copies:
        copy.start()
    for copy in copies:
        copy.wait()


def stored(arrays):
    anywhere = pl.BlockSpec(memory_space=pl.ANY)
    return pl.pallas_call(
        stored_kernel,
        out_shape=[jax.ShapeDtypeStruct(a.shape, a.dtype) for a in arrays],
        in_specs=[pl.BlockSpec(memory_space=pltpu.VMEM)] * 3,
        out_specs=[anywhere] * 3,
        scratch_shapes=[pltpu.SemaphoreType.DMA((3, arrays[0].shape[0]))],
        compiler_params=pltpu.CompilerParams(vmem_limit_bytes=2**20),
        name="stored",
    )(*arrays)


def on_grid(fields, flat_gain):
    x = jnp.transpose(fields[0], (1, 2, 0))
    gain = jnp.transpose(flat_gain, (1, 0, 2))
    corrected, illumination, mean_field = stored(fused(x, gain, lax.axis_size("strip")))
    back = lambda a: jnp.transpose(a, (1, 0, 2))
    return (jnp.transpose(corrected, (2, 0, 1))[None], back(illumination), back(mean_field))


def on_device(fields, flat_gain):
    num_fields, height, channels, width = fields.shape
    strips = lax.axis_size("strip")
    plates = lax.axis_size("plate")
    strip_rows = height // strips
    count = num_fields * strips * plates
    block = fields
    partial_sum = lax.psum_scatter(
        jnp.sum(block, axis=0, dtype=jnp.float32), "strip", scatter_dimension=0, tiled=True
    )
    total = lax.psum(partial_sum, "plate")
    mean_field = total / count
    col_index = jnp.arange(width, dtype=jnp.float32)
    col_kernel = gauss_weights(col_index, col_index, float(width))
    smooth_cols = jnp.einsum("hcv,wv->hcw", mean_field, col_kernel, precision=lax.Precision.HIGHEST)
    padded = padded_2(smooth_cols, (("strip", 0),), RADIUS)
    first_row = (lax.axis_index("strip") * strip_rows).astype(jnp.float32)
    out_index = first_row + jnp.arange(strip_rows, dtype=jnp.float32)
    in_index = first_row - RADIUS + jnp.arange(strip_rows + 2 * RADIUS, dtype=jnp.float32)
    row_kernel = gauss_weights(out_index, in_index, float(height))
    illumination = jnp.einsum("hu,ucw->hcw", row_kernel, padded, precision=lax.Precision.HIGHEST)
    illum_round = (illumination * flat_gain.astype(jnp.float32)).astype(jnp.bfloat16)
    block = fields
    corrected = (
        block.astype(jnp.float32)
        / lax.all_gather(illum_round, "strip", axis=0, tiled=True).astype(jnp.float32)[None]
    ).astype(jnp.bfloat16)
    return (corrected, illumination, mean_field)


def solution(mesh):
    grid = mesh.shape["strip"] == 8 and mesh.shape["plate"] == 2
    return jax.shard_map(
        on_grid if grid else on_device,
        mesh=mesh,
        in_specs=(P(("batch", "strip", "plate"), None, None, None), P("strip", None, None)),
        out_specs=(
            P(("batch", "strip", "plate"), None, None, None),
            P("strip", "batch", None),
            P("strip", "batch", None),
        ),
        check_vma=False,
    )
```

```python
import functools
import jax
import jax.numpy as jnp
import numpy as np
from jax import lax
from jax.experimental import pallas as pl
from jax.experimental.pallas import tpu as pltpu
from jax.sharding import PartitionSpec as P

SIGMA = 16
RADIUS = 48
ROWS = 8
WIDE = 256
REACH = 512
LANES = 128
CHUNK = 40
MESH = pl.DeviceIdType.MESH
LINK = jnp.bfloat16


def coded(mean):
    for _ in range(4):
        mean = mean * mean
    return mean.astype(LINK)


def decoded(code):
    code = code.astype(jnp.float32)
    for _ in range(4):
        code = lax.rsqrt(code)
    return code


def padded_2(array, sides, width):
    for axis, dim in sides:
        count, length = (lax.axis_size(axis), array.shape[dim])
        up = [(i, (i + 1) % count) for i in range(count - 1)]
        down = [(j, i) for i, j in up]
        last = lax.slice_in_dim(array, length - width, length, axis=dim)
        first = lax.slice_in_dim(array, 0, width, axis=dim)
        before = lax.ppermute(last, axis, up)
        after = lax.ppermute(first, axis, down)
        array = jnp.concatenate([before, array, after], axis=dim)
    return array


def gauss_weights(out_index, in_index, length):
    offset = out_index[:, None] - in_index[None, :]
    inside = (jnp.abs(offset) <= RADIUS) & (in_index[None, :] >= 0.0) & (in_index[None, :] < length)
    weights = jnp.where(inside, jnp.exp(-offset * offset / (2.0 * SIGMA * SIGMA)), 0.0)
    return weights / jnp.sum(weights, axis=1, keepdims=True)


def gauss_table(length):
    index = np.arange(length, dtype=np.float64)
    offset = index[:, None] - index[None, :]
    weights = np.where(np.abs(offset) <= RADIUS, np.exp(-offset * offset / (2.0 * SIGMA * SIGMA)), 0.0)
    return weights / np.sum(weights, axis=1, keepdims=True)


def halves(table):
    table = table.astype(np.float32)
    high = table.astype(jnp.bfloat16)
    low = (table - high.astype(np.float32)).astype(jnp.bfloat16)
    return np.stack([high, low])


def row_tables(height, strips):
    rows = height // strips
    gap = -rows % 16
    table = np.pad(gauss_table(height), ((0, 0), (RADIUS, RADIUS)))
    out = []
    for s in range(strips):
        own = table[s * rows:(s + 1) * rows]
        first = s * rows + RADIUS
        out.append(halves(np.concatenate([
            own[:, first:first + rows], np.zeros((rows, gap)),
            own[:, first - RADIUS:first], own[:, first + rows:first + rows + RADIUS]], axis=1)))
    return np.stack(out)


def column_tiles(width):
    padded = -(-width // LANES) * LANES
    table = np.pad(gauss_table(width).T, ((0, padded - width), (0, padded + WIDE - width)))
    tables, plan = [], []
    for w in range(0, padded, WIDE):
        start = min(max(w - LANES, 0), padded - REACH)
        block = halves(table[start:start + REACH, w:w + WIDE])
        same = [i for i, other in enumerate(tables) if np.array_equal(block, other)]
        if not same:
            tables.append(block)
        plan.append((w, min(WIDE, padded - w), min(WIDE, width - w), start, same[0] if same else len(tables) - 1))
    return np.stack(tables), plan


def split(value):
    high = value.astype(jnp.bfloat16)
    return high, (value - high.astype(jnp.float32)).astype(jnp.bfloat16)


def product(a, b):
    dot = functools.partial(jnp.dot, preferred_element_type=jnp.float32)
    return dot(a[0], b[0]) + (dot(a[0], b[1]) + dot(a[1], b[0]))


def at(strip, plate):
    return {"strip": strip, "plate": plate}


def levels_first(c):
    return c == 2


def packing(rows, width):
    full, rest = divmod(width, LANES)
    fold = -(-rows // 16) * 8
    return full, rest, fold, full * rows + fold


def unpack(rows, width, get, put):
    full, rest, fold, _ = packing(rows, width)
    for j in range(full):
        put(pl.ds(0, rows), pl.ds(j * LANES, LANES), get(pl.ds(j * rows, rows)))
    tail = get(pl.ds(full * rows, fold))
    at_rest = pl.ds(full * LANES, rest)
    put(pl.ds(0, fold), at_rest, tail[:, :rest])
    put(pl.ds(fold, rows - fold), at_rest, pltpu.roll(tail, LANES // 2, 1)[:rows - fold, :rest])


def quotient(turned, c, rows, x_ref, out_ref):
    strips, width = turned.shape[1] * 2, x_ref.shape[1]
    full, rest, fold, _ = packing(rows, width)

    def part(at_w, below):
        out_ref[at_w, :] = (x_ref[c, at_w, :].astype(jnp.float32) / below).astype(out_ref.dtype)

    for j in range(full):
        block = turned[c, :, :, pl.ds(j * rows, rows), :].reshape(strips * rows, LANES)
        part(pl.ds(j * LANES, LANES), jnp.transpose(block).astype(jnp.float32))
    pieces = []
    for k in range(strips):
        tail = turned[c, k // 2, k % 2, pl.ds(full * rows, fold), :].astype(jnp.float32)
        pieces += [tail, pltpu.roll(tail, LANES // 2, 1)[:rows - fold]]
    part(pl.ds(full * LANES, rest), jnp.transpose(jnp.concatenate(pieces, axis=0))[:rest])


def fused_kernel(plan, x_ref, gain_ref, kh_ref, kw_ref, out_ref, illum_ref, mean_ref, turned,
                 sib, ybuf, zbuf, halo, gain, kh, kw, padded, rowed, partial, edge,
                 load_sem, weight_sem, freed, sib_send, sib_recv, y_send, y_recv, z_send, z_recv,
                 h_send, h_recv, m_send, m_recv, i_send, i_recv, g_send, g_recv):
    channels, rows, width = mean_ref.shape
    nz = turned.shape[1]
    full, rest, fold, depth = packing(rows, width)
    chunks = [pl.ds(r, min(CHUNK, depth - r)) for r in range(0, depth, CHUNK)]
    strips = nz * 2
    strip, plate = lax.axis_index("strip"), lax.axis_index("plate")
    y, z = lax.rem(strip, 2), lax.div(strip, 2)
    owner = y == plate
    smoother = jnp.logical_not(owner)
    line = 1 - plate
    has_before, has_after = strip >= 1, strip + 1 < strips
    sibling, across = at(strip, 1 - plate), at(z * 2 + 1 - y, plate)
    diagonal = at(lax.rem(strip + 2 * y - 1 + strips, strips), plate)
    gap = padded.shape[1] - 2 * RADIUS
    upper, lower = at(lax.rem(strip + 2, strips), plate), at(lax.rem(strip + strips - 2, strips), plate)

    def remote(src, dst, send, recv, target):
        return pltpu.make_async_remote_copy(src, dst, send, recv, device_id=target, device_id_type=MESH)

    def load(c):
        return pltpu.make_async_copy(x_ref.at[c], out_ref.at[c], load_sem.at[c])

    def weights():
        return [pltpu.make_async_copy(gain_ref, gain, weight_sem.at[0]),
                pltpu.make_async_copy(kh_ref.at[strip], kh, weight_sem.at[1]),
                pltpu.make_async_copy(kw_ref, kw, weight_sem.at[2])]

    def to_sibling(c):
        return remote(turned.at[c, :, 1 - plate], sib.at[c], sib_send.at[c], sib_recv.at[c], sibling)

    def over(c, k):
        return remote(sib.at[c, k], ybuf.at[c, k], y_send.at[c, k], y_recv.at[c, k], across)

    def turn_of(i):
        down = nz - 1 - i
        return jnp.where(z * 2 < nz, down - (down <= z).astype(jnp.int32), i + (i >= z).astype(jnp.int32))

    def chain(c, k, up):
        slot = k + 1 if up else k
        return remote(sib.at[c, k], zbuf.at[c, slot], z_send.at[c, slot], z_recv.at[c, slot],
                      upper if up else lower)

    def halo_up(c):
        return remote(halo.at[c, 1], halo.at[c, 0], h_send.at[c, 1], h_recv.at[c, 0],
                      at(lax.rem(strip + 1, strips), plate))

    def halo_down(c):
        return remote(halo.at[c, 0], halo.at[c, 1], h_send.at[c, 0], h_recv.at[c, 1],
                      at(lax.rem(strip + strips - 1, strips), plate))

    def share_mean(c):
        return remote(mean_ref.at[c], mean_ref.at[c], m_send.at[c], m_recv.at[c], sibling)

    def share_illum(c):
        return remote(illum_ref.at[c], illum_ref.at[c], i_send.at[c], i_recv.at[c], sibling)

    def gather(c, k, kind):
        target = (sibling, across, upper, lower)[kind]
        slot = turned.at[c, k, line]
        return remote(slot, slot, g_send.at[c, k, kind], g_recv.at[c, k, line], target)

    def gathered(c, k):
        slot = turned.at[c, k, plate]
        return remote(slot, slot, g_send.at[c, k, 0], g_recv.at[c, k, plate], sibling)

    def turn(c):
        load(c).wait()
        for j in range(full):
            block = jnp.transpose(out_ref[c, pl.ds(j * LANES, LANES), :])
            for k in range(strips):
                turned[c, k // 2, k % 2, pl.ds(j * rows, rows), :] = block[k * rows:(k + 1) * rows]
        near = full * LANES - LANES // 2
        both = jnp.transpose(out_ref[c, pl.ds(near, width - near), :])
        ends = jnp.transpose(out_ref[c, pl.ds(full * LANES, rest), :])
        for k in range(strips):
            slot = turned.at[c, k // 2, k % 2]
            slot[pl.ds(full * rows, rows - fold), pl.ds(0, width - near)] = both[k * rows + fold:(k + 1) * rows]
            slot[pl.ds(full * rows, fold), pl.ds(0, rest)] = ends[k * rows:k * rows + fold]

    def paired(c, k, at_r):
        return turned[c, k, plate, at_r, :].astype(jnp.float32) + sib[c, k, at_r, :].astype(jnp.float32)

    def release(c):
        to_sibling(c).wait_send()
        pl.semaphore_signal(freed.at[c], inc=1, device_id=sibling, device_id_type=MESH)

    def encode(c):
        to_sibling(c).wait_recv()
        release(c)

        def strip_sum(k):
            for at_r in chunks:
                sib[c, k, at_r, :] = coded(paired(c, k, at_r) * 0.5)

        @pl.loop(0, nz)
        def _(i):
            k = jnp.where(i < nz - 1, turn_of(i), z)
            strip_sum(k)
            pl.when(i == 0)(lambda: pl.semaphore_wait(freed.at[c], 1))
            over(c, k).start()

    def summed(c, k, at_r):
        return paired(c, k, at_r) + 2.0 * decoded(ybuf[c, k, at_r, :])

    def pass_on(c, count, term):
        def passed_on(k, up):
            levels = z if up else nz - 1 - z
            before = count * levels.astype(jnp.float32)
            scale = 1.0 / (before + count)

            @pl.when(levels > 0)
            def _():
                chain(c, k, up).wait_recv()
                for at_r in chunks:
                    value = term(c, k, at_r) + before * decoded(zbuf[c, k + 1 if up else k, at_r, :])
                    sib[c, k, at_r, :] = coded(value * scale)

            @pl.when(levels == 0)
            def _():
                for at_r in chunks:
                    sib[c, k, at_r, :] = coded(term(c, k, at_r) * scale)

            chain(c, k, up).start()

        @pl.loop(0, nz - 1)
        def _(i):
            k = turn_of(i)
            if term is summed:
                over(c, k).wait_recv()
            pl.when(k > z)(lambda: passed_on(k, True))
            pl.when(k < z)(lambda: passed_on(k, False))

    def into_mean(c, get):
        def put(at_r, cols, value):
            mean_ref[c, at_r, cols] = value

        unpack(rows, width, get, put)

    def onto_mean(c, get):
        def put(at_r, cols, value):
            mean_ref[c, at_r, cols] += value

        unpack(rows, width, get, put)

    def onto_partial(c, get):
        for at_r in chunks:
            partial[at_r, :] += get(at_r)

    def add_levels(c, count, onto):
        def add(up):
            chain(c, z, up).wait_recv()
            weight = count * (z if up else nz - 1 - z).astype(jnp.float32)
            onto(c, lambda at_r: weight * decoded(zbuf[c, z + 1 if up else z, at_r, :]))

        pl.when(z >= 1)(lambda: add(True))
        pl.when(z + 1 < nz)(lambda: add(False))

    def pass_column(c):
        to_sibling(c).wait_recv()
        pl.when(smoother)(lambda: release(c))
        pl.semaphore_wait(freed.at[c], 1)
        pass_on(c, 2.0, paired)

    def column_sums(c):
        pass_column(c)
        into_mean(c, lambda at_r: paired(c, z, at_r))

    def encode_column(c):
        pass_column(c)
        for at_r in chunks:
            partial[at_r, :] = paired(c, z, at_r)
        add_levels(c, 2.0, onto_partial)
        for at_r in chunks:
            sib[c, z, at_r, :] = coded(partial[at_r, :] * (1.0 / strips))
        over(c, z).start()

    def across_sums(c):
        to_sibling(c).wait_recv()
        pl.semaphore_wait(freed.at[c], 1)
        pass_on(c, 4.0, summed)
        over(c, z).wait_recv()
        into_mean(c, lambda at_r: summed(c, z, at_r))

    def finish_mean(c):
        pl.when(jnp.logical_not(levels_first(c)))(lambda: add_levels(c, 4.0, onto_mean))

        @pl.when(levels_first(c))
        def _():
            add_levels(c, 2.0, onto_mean)
            over(c, z).wait_recv()
            onto_mean(c, lambda at_r: strips * decoded(ybuf[c, z, at_r, :]))

        for r in range(0, rows, ROWS):
            at_r = pl.ds(r, ROWS)
            value = mean_ref[c, at_r, :]
            value = value * (1.0 / (2 * strips))
            mean_ref[c, at_r, :] = value
            if r < RADIUS:
                halo[c, 0, at_r, :] = coded(value)
            if r >= rows - RADIUS:
                halo[c, 1, pl.ds(r - rows + RADIUS, ROWS), :] = coded(value)
        pl.when(has_after)(lambda: halo_up(c).start())
        pl.when(has_before)(lambda: halo_down(c).start())
        share_mean(c).start()

    def fill(r, value):
        at_r = pl.ds(r, value.shape[0])
        high, low = split(value)
        padded[0, at_r, pl.ds(0, width)] = high
        padded[1, at_r, pl.ds(0, width)] = low

    def smooth(c):
        share_mean(c).wait_recv()
        for r in range(0, rows, ROWS):
            fill(r, mean_ref[c, pl.ds(r, ROWS), :])

        @pl.when(has_before)
        def _():
            halo_up(c).wait_recv()
            for r in range(0, RADIUS, ROWS):
                fill(gap + r, decoded(halo[c, 0, pl.ds(r, ROWS), :]))

        @pl.when(has_after)
        def _():
            halo_down(c).wait_recv()
            for r in range(0, RADIUS, ROWS):
                fill(gap + RADIUS + r, decoded(halo[c, 1, pl.ds(r, ROWS), :]))

        for w, wide, _, _, _ in plan:
            cols = pl.ds(w, wide)
            value = product((kh[0], kh[1]), (padded[0, :, cols], padded[1, :, cols]))
            rowed[0, :, cols], rowed[1, :, cols] = split(value)

        for w, wide, used, start, index in plan:
            reach = pl.ds(start, REACH)
            value = product((rowed[0, :, reach], rowed[1, :, reach]),
                            (kw[index, 0, :, pl.ds(0, wide)], kw[index, 1, :, pl.ds(0, wide)]))[:, :used]
            cols = pl.ds(w, used)
            illum_ref[c, :, cols] = value
            weighted = value * gain[c, :, cols].astype(jnp.float32)
            for j in range(w // LANES, (w + used) // LANES):
                tile = weighted[:, j * LANES - w:(j + 1) * LANES - w]
                turned[c, z, y, pl.ds(j * rows, rows), :] = tile.astype(jnp.bfloat16)
            if used % LANES:
                edge[:, pl.ds(0, rest)] = weighted[:, used - rest:]
                moved = pltpu.roll(edge[pl.ds(fold, rows - fold), :], LANES // 2, 1)
                slot = turned.at[c, z, y]
                slot[pl.ds(full * rows, rows - fold), :] = moved.astype(jnp.bfloat16)
                slot[pl.ds(full * rows, fold), pl.ds(0, rest)] = edge[pl.ds(0, fold), pl.ds(0, rest)].astype(jnp.bfloat16)
        pl.when(z + 1 < nz)(lambda: gather(c, z, 2).start())
        pl.when(z >= 1)(lambda: gather(c, z, 3).start())
        gather(c, z, 1).start()
        gather(c, z, 0).start()
        share_illum(c).start()

    def relay(c):
        @pl.loop(0, nz)
        def _(d):
            @pl.when((z - d >= 0) & ((d > 0) | owner))
            def _():
                k = z - d
                gather(c, k, 0).wait_recv()
                pl.when(smoother & (z + 1 < nz))(lambda: gather(c, k, 2).start())
                pl.when(smoother)(lambda: gather(c, k, 1).start())
                gather(c, k, 0).start()

            @pl.when((z + d < nz) & (d > 0))
            def _():
                k = z + d
                gather(c, k, 0).wait_recv()
                pl.when(smoother & (z >= 1))(lambda: gather(c, k, 3).start())
                pl.when(smoother)(lambda: gather(c, k, 1).start())
                gather(c, k, 0).start()

    def divide(c):
        @pl.loop(0, nz)
        def _(k):
            gathered(c, k).wait_recv()

        quotient(turned, c, rows, out_ref, out_ref.at[c])

    partners = [sibling, across, diagonal] + [upper, lower]
    load(0).start()
    barrier = pltpu.get_barrier_semaphore()
    for partner in partners:
        pl.semaphore_signal(barrier, inc=1, device_id=partner, device_id_type=MESH)
    load(1).start()
    turn(0)
    pl.semaphore_wait(barrier, len(partners))
    to_sibling(0).start()
    for c in range(2, channels):
        load(c).start()
    for copy in weights():
        copy.start()

    def order(t):
        return t + (t == 2).astype(jnp.int32) - (t == 3).astype(jnp.int32)

    def turn_and_send(c):
        turn(c)
        to_sibling(c).start()

    @pl.when(smoother)
    def _():
        padded[...] = jnp.zeros_like(padded)

        @pl.loop(0, channels)
        def _(t):
            pl.when(t + 1 < channels)(lambda: turn_and_send(t + 1))
            c = order(t)
            pl.when(levels_first(c))(lambda: encode_column(c))
            pl.when(jnp.logical_not(levels_first(c)))(lambda: encode(c))

        for copy in weights():
            copy.wait()

        @pl.loop(0, channels + 2)
        def _(c):
            pl.when(c < channels)(lambda: smooth(c))
            pl.when((c >= 1) & (c <= channels))(lambda: relay(c - 1))
            pl.when(c >= 2)(lambda: divide(c - 2))

    @pl.when(owner)
    def _():
        @pl.loop(1, channels + 1)
        def _(c):
            pl.when(c < channels)(lambda: turn_and_send(c))
            release(c - 1)

        @pl.loop(0, channels * 2)
        def _(c):
            pl.when((c < channels) & jnp.logical_not(levels_first(c)))(lambda: across_sums(c))
            pl.when((c < channels) & levels_first(c))(lambda: column_sums(c))
            pl.when((c >= 1) & (c <= channels))(lambda: finish_mean(c - 1))
            pl.when((c >= 4) & (c < channels + 4))(lambda: relay(c - 4))
            pl.when((c >= 5) & (c < channels + 3))(lambda: divide(c - 5))
            pl.when((c >= channels + 2) & (c < channels + 4))(lambda: divide(c - 4))

        for copy in weights():
            copy.wait()

        @pl.loop(0, channels)
        def _(c):
            share_illum(c).wait_recv()

    @pl.loop(0, channels)
    def _(c):
        @pl.when(smoother)
        def _():
            share_illum(c).wait_send()

            @pl.loop(0, nz)
            def _(k):
                pl.when((k == z) | jnp.logical_not(levels_first(c)))(lambda: over(c, k).wait_send())

        @pl.when(owner)
        def _():
            share_mean(c).wait_send()
            pl.when(has_after)(lambda: halo_up(c).wait_send())
            pl.when(has_before)(lambda: halo_down(c).wait_send())

        chained = owner | levels_first(c)

        @pl.loop(0, nz)
        def _(k):
            pl.when(chained & (k > z))(lambda: chain(c, k, True).wait_send())
            pl.when(chained & (k < z))(lambda: chain(c, k, False).wait_send())
            gather(c, k, 0).wait_send()
            pl.when(smoother)(lambda: gather(c, k, 1).wait_send())
            pl.when(smoother & (k <= z) & (z + 1 < nz))(lambda: gather(c, k, 2).wait_send())
            pl.when(smoother & (k >= z) & (z >= 1))(lambda: gather(c, k, 3).wait_send())


def fused(x, gain, strips):
    channels, width, height = x.shape
    rows, nz = height // strips, strips // 2
    padded_width = -(-width // LANES) * LANES
    kh = row_tables(height, strips)
    kw, plan = column_tiles(width)
    dma = pltpu.SemaphoreType.DMA
    each, levels, chains = dma((channels,)), dma((channels, nz)), dma((channels, nz + 1))
    depth = packing(rows, width)[3]
    part = (channels, nz, depth, LANES)
    own = (channels, rows, width)
    anywhere = pl.BlockSpec(memory_space=pl.ANY)
    held = [pltpu.VMEM(x.shape, x.dtype), pltpu.VMEM(own, jnp.float32), pltpu.VMEM(own, jnp.float32)]
    return pl.pallas_call(
        functools.partial(fused_kernel, plan),
        out_shape=held,
        in_specs=[anywhere] * 4,
        out_specs=[pl.BlockSpec(memory_space=pltpu.VMEM)] * 3,
        scratch_shapes=[
            pltpu.VMEM((channels, nz, 2, depth, LANES), x.dtype),
            pltpu.VMEM(part, LINK),
            pltpu.VMEM(part, LINK),
            pltpu.VMEM((channels, nz + 1, depth, LANES), LINK),
            pltpu.VMEM((channels, 2, RADIUS, width), LINK),
            pltpu.VMEM(own, gain.dtype),
            pltpu.VMEM(kh.shape[1:], jnp.bfloat16),
            pltpu.VMEM(kw.shape, jnp.bfloat16),
            pltpu.VMEM((2, kh.shape[3], padded_width), jnp.bfloat16),
            pltpu.VMEM((2, rows, padded_width), jnp.bfloat16),
            pltpu.VMEM((depth, LANES), jnp.float32),
            pltpu.VMEM((rows, LANES), jnp.float32),
            each, dma((3,)), pltpu.SemaphoreType.REGULAR((channels,)), each, each, levels, levels, chains, chains,
            dma((channels, 2)), dma((channels, 2)), each, each, each, each,
            dma((channels, nz, 4)), dma((channels, nz, 2)),
        ],
        compiler_params=pltpu.CompilerParams(
            collective_id=0, has_side_effects=True, vmem_limit_bytes=45 * 2**20),
        name="fused",
    )(x, gain, kh, kw)


def stored_kernel(*refs):
    sources, targets, sems = refs[:3], refs[3:6], refs[6]
    copies = [pltpu.make_async_copy(source.at[c], target.at[c], sems.at[i, c])
              for i, (source, target) in enumerate(zip(sources, targets)) for c in range(source.shape[0])]
    for copy in copies:
        copy.start()
    for copy in copies:
        copy.wait()


def stored(arrays):
    anywhere = pl.BlockSpec(memory_space=pl.ANY)
    return pl.pallas_call(
        stored_kernel,
        out_shape=[jax.ShapeDtypeStruct(a.shape, a.dtype) for a in arrays],
        in_specs=[pl.BlockSpec(memory_space=pltpu.VMEM)] * 3,
        out_specs=[anywhere] * 3,
        scratch_shapes=[pltpu.SemaphoreType.DMA((3, arrays[0].shape[0]))],
        compiler_params=pltpu.CompilerParams(vmem_limit_bytes=2**20),
        name="stored",
    )(*arrays)


def on_grid(fields, flat_gain):
    x = jnp.transpose(fields[0], (1, 2, 0))
    gain = jnp.transpose(flat_gain, (1, 0, 2))
    corrected, illumination, mean_field = stored(fused(x, gain, lax.axis_size("strip")))
    back = lambda a: jnp.transpose(a, (1, 0, 2))
    return (jnp.transpose(corrected, (2, 0, 1))[None], back(illumination), back(mean_field))


def on_device(fields, flat_gain):
    num_fields, height, channels, width = fields.shape
    strips = lax.axis_size("strip")
    plates = lax.axis_size("plate")
    strip_rows = height // strips
    count = num_fields * strips * plates
    block = fields
    partial_sum = lax.psum_scatter(
        jnp.sum(block, axis=0, dtype=jnp.float32), "strip", scatter_dimension=0, tiled=True
    )
    total = lax.psum(partial_sum, "plate")
    mean_field = total / count
    col_index = jnp.arange(width, dtype=jnp.float32)
    col_kernel = gauss_weights(col_index, col_index, float(width))
    smooth_cols = jnp.einsum("hcv,wv->hcw", mean_field, col_kernel, precision=lax.Precision.HIGHEST)
    padded = padded_2(smooth_cols, (("strip", 0),), RADIUS)
    first_row = (lax.axis_index("strip") * strip_rows).astype(jnp.float32)
    out_index = first_row + jnp.arange(strip_rows, dtype=jnp.float32)
    in_index = first_row - RADIUS + jnp.arange(strip_rows + 2 * RADIUS, dtype=jnp.float32)
    row_kernel = gauss_weights(out_index, in_index, float(height))
    illumination = jnp.einsum("hu,ucw->hcw", row_kernel, padded, precision=lax.Precision.HIGHEST)
    illum_round = (illumination * flat_gain.astype(jnp.float32)).astype(jnp.bfloat16)
    block = fields
    corrected = (
        block.astype(jnp.float32)
        / lax.all_gather(illum_round, "strip", axis=0, tiled=True).astype(jnp.float32)[None]
    ).astype(jnp.bfloat16)
    return (corrected, illumination, mean_field)


def solution(mesh):
    grid = mesh.shape["strip"] == 8 and mesh.shape["plate"] == 2
    return jax.shard_map(
        on_grid if grid else on_device,
        mesh=mesh,
        in_specs=(P(("batch", "strip", "plate"), None, None, None), P("strip", None, None)),
        out_specs=(
            P(("batch", "strip", "plate"), None, None, None),
            P("strip", "batch", None),
            P("strip", "batch", None),
        ),
        check_vma=False,
    )
```
